512 devices in a mesh: tm: 16 (over z), lon: 32 (over y, x, core).
Axes of the slice: x: 4, y: 4, z: 16, core: 2. Of those that a mesh axis runs over, the one named last changes fastest.
Arguments:
- noise: bfloat16 [2, 256, 1024, 512], P(None, 'tm', 'lon'), may hold values from -6 to 6
- observed: float32 [256, 256, 1024], P('tm', 'lon'), may hold values from -6 to 6
- mask: int32 [256, 256, 1024], P('tm', 'lon'), may hold values from 0 to 1, as said below
- lat_factor: bfloat16 [256, 256], replicated, as said below
- lon_factor: bfloat16 [1024, 1024], P('lon'), as said below
- spectrum: float32 [257], replicated, may hold values from 0.1 to 4
Outputs:
- posterior: float32 [2, 256, 256, 1024], P(None, 'tm', 'lon')
- residual_next: float32 [2, 256, 256, 1024], P(None, 'tm', 'lon')
The draws below stay inside these ranges and needn't reach their ends.
Inputs may be any that keep to these rules, and one draw needn't show every extreme that they name: `mask`: 1 where the cell is observed, 0 elsewhere. `lat_factor`: lower triangular with a positive diagonal. `lon_factor`: lower triangular with a positive diagonal.
All inputs are finite; a program needn't handle non-finite values.
Results may differ from the reference program's by a relative error of at most 0.0026.
Values may be sent and summed in bfloat16 or wider, within the bound.
A program may use at most 64 MiB of HBM per device.

```python
import math
import jax
import jax.numpy as jnp
from jax import lax

LON = 1024
LAT = 256
HOURS = 256
EMBED = 512


def lower_factor(key, order):
    entries = jax.random.normal(jax.random.fold_in(key, 11), (order, order), jnp.float32)
    diagonal = jax.random.uniform(jax.random.fold_in(key, 12), (order,), jnp.float32, 0.5, 1.0)
    row_index = lax.broadcasted_iota(jnp.int32, (order, order), 0)
    col_index = lax.broadcasted_iota(jnp.int32, (order, order), 1)
    scaling = jnp.sqrt(0.5 / (row_index + 1).astype(jnp.float32))
    lower = jnp.where(col_index < row_index, entries * scaling, 0.0)
    return lower + jnp.where(col_index == row_index, diagonal[:, None], 0.0)


def draw_lat_factor(key, part):
    return lower_factor(key, LAT).astype(jnp.bfloat16)


def draw_lon_factor(key, part):
    return lower_factor(key, LON).astype(jnp.bfloat16)


def draw_mask(key, part):
    ticket = jax.random.randint(jax.random.fold_in(key, 21), (HOURS, LAT, LON), 0, 1000)
    hour_index = lax.broadcasted_iota(jnp.int32, (HOURS, LAT, LON), 0)
    lat_index = lax.broadcasted_iota(jnp.int32, (HOURS, LAT, LON), 1)
    limit = 200 + 350 * hour_index // (HOURS - 1) + 350 * lat_index // (LAT - 1)
    return jnp.where(ticket < limit, 1, 0).astype(jnp.int32)


def block_scale(own_key, dims, shards, least, high):
    level, own = 1.0, jax.random.fold_in(own_key, 6)
    for dim, parts in shards:
        draws = jnp.exp(jax.random.uniform(jax.random.fold_in(own, dim), (parts,), jnp.float32, least / len(shards), high / len(shards)))
        level = level * jnp.repeat(draws, dims[dim] // parts).reshape([-1 if axis == dim else 1 for axis in range(len(dims))])
    return level


def centred(rng, extent, deviation, most, pieces=(), kind=jnp.bfloat16):
    values = jax.random.normal(rng, extent, jnp.float32) * deviation
    if len(pieces) > 0:
        values = block_scale(rng, extent, pieces, -0.22, 0.18) * values
    return jnp.clip(values, min=-most, max=most).astype(kind)


def setup_inputs(seed: int = 0) -> dict:
    splits = jax.random.split(jax.random.key(seed), 7)
    noise = centred(splits[0], (2, LAT, LON, EMBED), 1.0, 6.0, ((1, 16), (2, 32)))
    observed = centred(splits[1], (HOURS, LAT, LON), 1.0, 6.0, ((0, 16), (1, 32)), jnp.float32)
    mask = draw_mask(jax.random.fold_in(splits[6], 71), 0)
    lat_factor = draw_lat_factor(jax.random.fold_in(splits[6], 71), 0)
    lon_factor = draw_lon_factor(jax.random.fold_in(splits[6], 71), 0)
    spectrum = jnp.clip(jnp.exp(jax.random.uniform(splits[5], (HOURS + 1,), jnp.float32, math.log(0.1), math.log(4.0))), 0.1, 4.0)
    return {"noise": noise, "observed": observed, "mask": mask, "lat_factor": lat_factor, "lon_factor": lon_factor, "spectrum": spectrum}


PRECISE = lax.Precision.HIGHEST
NOISE_VAR = 0.25

def reference(noise, observed, mask, lat_factor, lon_factor, spectrum):
    periods = 2 * HOURS
    powers = jnp.concatenate([spectrum, spectrum[1:-1][::-1]])
    amplitude = jnp.sqrt(powers / periods)
    row_index = lax.broadcasted_iota(jnp.int32, (HOURS, periods), 0)
    col_index = lax.broadcasted_iota(jnp.int32, (HOURS, periods), 1)
    phase = (row_index * col_index % periods).astype(jnp.float32) * (2.0 * jnp.pi / periods)
    table_cos = (jnp.cos(phase) * amplitude).astype(jnp.bfloat16)
    table_sin = (jnp.sin(phase) * amplitude).astype(jnp.bfloat16)

    def transform_row(noise_row):
        real_part = jnp.dot(noise_row[0], table_cos.T, preferred_element_type=jnp.float32) + jnp.dot(noise_row[1], table_sin.T, preferred_element_type=jnp.float32)
        imag_part = jnp.dot(noise_row[1], table_cos.T, preferred_element_type=jnp.float32) - jnp.dot(noise_row[0], table_sin.T, preferred_element_type=jnp.float32)
        return jnp.stack([real_part, imag_part])
    hourly = lax.map(transform_row, jnp.moveaxis(noise, 1, 0))
    hourly = jnp.transpose(hourly, (1, 3, 0, 2))
    lat_whole = lat_factor.astype(jnp.float32)
    lon_whole = lon_factor.astype(jnp.float32)
    prior_draw = jnp.einsum('ab,shbo->shao', lat_whole, hourly, precision=PRECISE)
    prior_draw = jnp.einsum('op,shap->shao', lon_whole, prior_draw, precision=PRECISE)
    observed_mask = mask.astype(jnp.float32)
    residual = observed_mask * (observed[None] - prior_draw)
    lat_kernel = jnp.dot(lat_whole, lat_whole.T, precision=PRECISE)
    lon_kernel = jnp.dot(lon_whole, lon_whole.T, precision=PRECISE)
    correlation = jnp.real(jnp.fft.ifft(powers))[:HOURS]
    hour_index = jnp.arange(HOURS)
    lag_table = jnp.abs(hour_index[:, None] - hour_index[None, :])
    hour_kernel = correlation[lag_table]
    applied = jnp.einsum('op,shap->shao', lon_kernel, residual, precision=PRECISE)
    applied = jnp.einsum('ab,shbo->shao', lat_kernel, applied, precision=PRECISE)
    applied = jnp.einsum('hk,skao->shao', hour_kernel, applied, precision=PRECISE)
    operated = observed_mask * applied + NOISE_VAR * residual
    norm_sq = lax.optimization_barrier(jnp.sum(residual * residual, axis=(1, 2, 3)))
    bending = lax.optimization_barrier(jnp.sum(residual * operated, axis=(1, 2, 3)))
    step_size = (norm_sq / bending)[:, None, None, None]
    return (prior_draw + step_size * applied, residual - step_size * operated)
```

```python
import functools

import jax
import jax.numpy as jnp
import numpy as np
from jax import lax
from jax.experimental import pallas as pl
from jax.experimental.pallas import tpu as pltpu
from jax.sharding import PartitionSpec as P

F32 = jnp.float32
BF16 = jnp.bfloat16
MESH = pl.DeviceIdType.MESH
NOISE_VAR = 0.25
NT = (((1,), (1,)), ((), ()))
NN = (((1,), (0,)), ((), ()))
HOPS = 8
ZN = 16
LN = 32


def dot(left, right, dims):
    return lax.dot_general(left, right, dims, preferred_element_type=F32)


def split(value):
    high = value.astype(BF16)
    return high, (value - high.astype(F32)).astype(BF16)


def exchange(parts, strides):
    parts = list(parts)
    lane = lax.broadcasted_iota(jnp.int32, parts[0].shape, 1)
    for bit, stride in enumerate(strides):
        low_lanes = (lane & stride) == 0
        for first in range(len(parts)):
            if first & (1 << bit):
                continue
            second = first | (1 << bit)
            low, high = parts[first], parts[second]
            parts[first] = jnp.where(low_lanes, low, pltpu.roll(high, stride, 1))
            parts[second] = jnp.where(low_lanes, pltpu.roll(low, 128 - stride, 1), high)
    return parts


def body(
    noise, obs_hbm, mask_hbm, lat, lon, amp, coarse, fine,
    post, nxt,
    obs, mask, tab, waves, work, ysc, ssc, lat32, latp, latq, latqt, hour,
    lonfull, halves, xd, prior, resid,
    send0, recv0, send1, recv1, send2, recv2, send3, recv3, send4, recv4, send5, recv5,
    redsend, redz, redmid, redl,
    send_sem, recv_sem, local_sem,
):
    mz = lax.axis_index("tm")
    ml = lax.axis_index("lon")

    def z_peer(step):
        away = (step // 2 + 1) * (1 - 2 * (step % 2))
        return lax.rem(mz + away + ZN, ZN)

    def l_peer(step):
        return lax.rem(ml + step + 1, LN)

    barrier = pltpu.get_barrier_semaphore()

    def greet_z(step, carry):
        pl.semaphore_signal(barrier, inc=1, device_id={"tm": z_peer(step)}, device_id_type=MESH)
        return carry

    def greet_l(step, carry):
        pl.semaphore_signal(barrier, inc=1, device_id={"lon": l_peer(step)}, device_id_type=MESH)
        return carry

    lax.fori_loop(0, ZN - 1, greet_z, 0)
    lax.fori_loop(0, LN - 1, greet_l, 0)
    obs_copy = pltpu.make_async_copy(obs_hbm, obs, local_sem.at[0])
    mask_copy = pltpu.make_async_copy(mask_hbm, mask, local_sem.at[1])
    obs_copy.start()
    mask_copy.start()

    def start_z(hop, s, src, dst):
        def one(step, carry):
            peer = z_peer(step)
            pltpu.make_async_remote_copy(
                src_ref=src.at[s, peer], dst_ref=dst.at[s, mz],
                send_sem=send_sem.at[hop, s], recv_sem=recv_sem.at[hop, s],
                device_id={"tm": peer}, device_id_type=MESH,
            ).start()
            return carry

        lax.fori_loop(0, ZN - 1, one, 0)
        dst[s, mz] = src[s, mz]

    def whole_z(hop, s, src, dst):
        return pltpu.make_async_remote_copy(
            src_ref=src.at[s, pl.ds(0, ZN - 1)], dst_ref=dst.at[s, pl.ds(0, ZN - 1)],
            send_sem=send_sem.at[hop, s], recv_sem=recv_sem.at[hop, s],
            device_id={"tm": z_peer(0)}, device_id_type=MESH,
        )

    def start_l(hop, s, src, dst):
        def one(step, carry):
            peer = l_peer(step)
            pltpu.make_async_remote_copy(
                src_ref=src.at[s, pl.ds(pl.multiple_of(peer * 32, 32), 32)],
                dst_ref=dst.at[s, pl.ds(pl.multiple_of(ml * 32, 32), 32)],
                send_sem=send_sem.at[hop, s], recv_sem=recv_sem.at[hop, s],
                device_id={"lon": peer}, device_id_type=MESH,
            ).start()
            return carry

        lax.fori_loop(0, LN - 1, one, 0)
        own = pl.ds(pl.multiple_of(ml * 32, 32), 32)
        dst[s, own] = src[s, own]

    def whole_l(hop, s, src, dst):
        rows = pl.ds(0, (LN - 1) * 32)
        return pltpu.make_async_remote_copy(
            src_ref=src.at[s, rows], dst_ref=dst.at[s, rows],
            send_sem=send_sem.at[hop, s], recv_sem=recv_sem.at[hop, s],
            device_id={"lon": l_peer(0)}, device_id_type=MESH,
        )

    amp_row = amp[...]

    def tables(group):
        base = pl.multiple_of(group * 8, 8)
        c1 = coarse[pl.ds(base, 8), :]
        s1 = coarse[pl.ds(16 + base, 8), :]
        for pair in range(8):
            cos_rows, sin_rows = [], []
            for hh in (2 * pair, 2 * pair + 1):
                c2, s2 = fine[hh : hh + 1, :], fine[16 + hh : 17 + hh, :]
                cos_rows.append((c1 * c2 - s1 * s2) * amp_row)
                sin_rows.append((s1 * c2 + c1 * s2) * amp_row)
            cw = jnp.concatenate(cos_rows, axis=0).astype(BF16)
            sw = jnp.concatenate(sin_rows, axis=0).astype(BF16)
            rows = pl.ds(pair * 16, 16)
            tab[0, group, rows, 0:512] = cw
            tab[0, group, rows, 512:1024] = sw
            tab[1, group, rows, 0:512] = -sw
            tab[1, group, rows, 512:1024] = cw

    def tables_loop(group, carry):
        tables(group)
        return carry

    lax.fori_loop(0, 2, tables_loop, 0)

    def transform(s):
        def one(group, carry):
            for part in range(2):
                rows = noise[part].reshape(512, 512)
                term = dot(rows, tab[s, group, :, part * 512 : (part + 1) * 512], NT)
                if part == 0:
                    work[0:512, :] = term
                else:
                    work[0:512, :] += term

            def swap(u, inner):
                parts = [work[pl.ds(u * 8 + og, 16, stride=32), :] for og in range(8)]
                parts = exchange(parts, (1, 2, 4))
                for jl in range(8):
                    send0[s, group * 8 + jl, u] = parts[jl].astype(BF16)
                return inner

            lax.fori_loop(0, 4, swap, 0)
            return carry

        lax.fori_loop(0, 2, one, 0)

    transform(0)
    pl.semaphore_wait(barrier, ZN + LN - 2)
    start_z(0, 0, send0, recv0)

    own_rows = pl.ds(pl.multiple_of(ml * 32, 32), 32)

    def gather(step, carry):
        pltpu.make_async_remote_copy(
            src_ref=lon, dst_ref=lonfull.at[own_rows],
            send_sem=local_sem.at[2], recv_sem=local_sem.at[3],
            device_id={"lon": l_peer(step)}, device_id_type=MESH,
        ).start()
        return carry

    lax.fori_loop(0, LN - 1, gather, 0)
    lonfull[own_rows, :] = lon[...]
    gathered = pltpu.make_async_remote_copy(
        src_ref=lonfull.at[pl.ds(0, 31 * 32)], dst_ref=lonfull.at[pl.ds(0, 31 * 32)],
        send_sem=local_sem.at[2], recv_sem=local_sem.at[3],
        device_id={"lon": l_peer(0)}, device_id_type=MESH,
    )
    transform(1)
    start_z(0, 1, send0, recv0)

    def spread(value):
        lat32[0:256, :] = value[:, 0:128]
        lat32[256:512, :] = value[:, 128:256]

    spread(lat[...].astype(F32))
    for k in range(8):
        latp[k * 32 : (k + 1) * 32, :] = jnp.concatenate(
            [lat32[pl.ds(c * 256 + k, 32, stride=8), :] for c in range(2)], axis=1
        ).astype(BF16)
    spread(latp[...].astype(F32).T)
    for bb in range(16):
        latqt[bb * 16 : (bb + 1) * 16, :] = jnp.concatenate(
            [lat32[pl.ds(c * 256 + bb, 16, stride=16), :] for c in range(2)], axis=1
        ).astype(BF16)
    latq[...] = latqt[...].astype(F32).T.astype(BF16)

    def wave(j, carry):
        c1 = coarse[pl.ds(j, 1), :] * amp_row
        s1 = coarse[pl.ds(16 + j, 1), :] * amp_row
        c2, s2 = fine[0:16, :], fine[16:32, :]
        rows = pl.ds(pl.multiple_of(j * 16, 16), 16)
        for part, value in enumerate((c1 * c2 - s1 * s2, s1 * c2 + c1 * s2)):
            high, low = split(value)
            waves[0, rows, part * 512 : (part + 1) * 512] = high
            waves[1, rows, part * 512 : (part + 1) * 512] = low
        return carry

    lax.fori_loop(0, ZN, wave, 0)
    cross = dot(waves[0], waves[1], NT)
    kernel = dot(waves[0], waves[0], NT) + (cross + cross.T)
    high, low = split(kernel)
    hour[0:256, :] = high
    hour[256:512, :] = low
    redsend[...] = jnp.zeros_like(redsend)
    obs_copy.wait()
    mask_copy.wait()

    def columns(index, width):
        return pl.ds(pl.multiple_of(index * width, width), width)

    def to_lon(s, dst):
        def swap(step, carry):
            u, lb = step // 2, step % 2
            parts = [
                ysc[pl.ds(pl.multiple_of(k * 32 + lb * 16, 16), 16), columns(u, 128)] for k in range(8)
            ]
            parts = exchange(parts, (1, 2, 4))
            for og in range(8):
                ssc[pl.ds(pl.multiple_of((u * 8 + og) * 32 + lb * 16, 16), 16), :] = parts[og]
            return carry

        lax.fori_loop(0, 8, swap, 0)

        def pick(peer, carry):
            dst[s, pl.ds(pl.multiple_of(peer * 32, 32), 32), :] = ssc[pl.ds(peer, 32, stride=32), :]
            return carry

        lax.fori_loop(0, LN, pick, 0)

    def lat_first(s):
        whole_z(0, s, send0, recv0).wait_recv()
        for u in range(4):
            ysc[:, u * 128 : (u + 1) * 128] = dot(latp[...], recv0[s, :, u].reshape(256, 128), NN)
        to_lon(s, send1)
        start_l(1, s, send1, recv1)

    def lon_columns(s, src):
        def turn(c, carry):
            block = src[s, columns(c, 128), :].T
            high, low = split(block)
            halves[0:128, columns(c, 128)] = high
            halves[128:256, columns(c, 128)] = low
            return carry

        lax.fori_loop(0, 8, turn, 0)

    def lon_first(s):
        whole_l(1, s, send1, recv1).wait_recv()
        lon_columns(s, recv1)

        def prior_block(n, total):
            both = dot(halves[...], lonfull[columns(n, 256), :], NT)
            drawn = both[0:128] + both[128:256]
            left = mask[:, columns(n, 256)].astype(F32) * (obs[:, columns(n, 256)] - drawn)
            prior[s, :, columns(n, 256)] = drawn
            resid[s, :, columns(n, 256)] = left
            squares = jnp.sum(left * left, axis=0, keepdims=True)
            return total + squares[:, 0:128] + squares[:, 128:256]

        redsend[s, 0:1, :] = lax.fori_loop(0, 4, prior_block, jnp.zeros((1, 128), F32))

        def halve(n, carry):
            high, low = split(resid[s, :, columns(n, 256)])
            halves[0:128, columns(n, 256)] = high
            halves[128:256, columns(n, 256)] = low
            return carry

        lax.fori_loop(0, 4, halve, 0)

        def back_block(n, carry):
            both = dot(halves[...], lonfull[:, columns(n, 256)], NN)
            summed = both[0:128] + both[128:256]
            for part in range(2):
                rows = pl.ds(pl.multiple_of(n * 256 + part * 128, 128), 128)
                send2[s, rows, :] = summed[:, part * 128 : (part + 1) * 128].T
            return carry

        lax.fori_loop(0, 4, back_block, 0)
        start_l(2, s, send2, recv2)

    def lat_back(s):
        whole_l(2, s, send2, recv2).wait_recv()

        def swap(step, carry):
            u, lb = step // 2, step % 2
            parts = [recv2[s, pl.ds(lb * 512 + u * 8 + pg, 16, stride=32), :] for pg in range(8)]
            parts = exchange(parts, (1, 2, 4))
            for k in range(8):
                high, low = split(parts[k])
                rows = pl.ds(pl.multiple_of(k * 32 + lb * 16, 16), 16)
                xd[0, rows, columns(u, 128)] = high
                xd[1, rows, columns(u, 128)] = low
            return carry

        lax.fori_loop(0, 8, swap, 0)
        for n in range(2):
            cols = slice(n * 256, (n + 1) * 256)
            ysc[:, cols] = dot(latqt[...], xd[0, :, cols], NN) + dot(latqt[...], xd[1, :, cols], NN)

        def turn(step, carry):
            u, ib = step // 2, step % 2
            parts = [ysc[pl.ds(pl.multiple_of(bb * 16 + ib * 8, 8), 8), columns(u, 128)] for bb in range(16)]
            parts = exchange(parts, (8, 16, 32, 64))
            for h in range(16):
                ssc[pl.ds(pl.multiple_of((u * 16 + h) * 16 + ib * 8, 8), 8), :] = parts[h]
            return carry

        lax.fori_loop(0, 8, turn, 0)

        def pick(peer, carry):
            for u in range(4):
                send3[s, peer, u] = ssc[pl.ds(u * 256 + peer, 16, stride=16), :].astype(BF16)
            return carry

        lax.fori_loop(0, ZN, pick, 0)
        start_z(3, s, send3, recv3)

    def hours_mix(s):
        whole_z(3, s, send3, recv3).wait_recv()
        total = jnp.zeros((1, 128), F32)
        for u in range(4):
            cells = recv3[s, :, u].reshape(256, 128)
            both = dot(hour[...], cells, NN)
            mixed = both[0:256] + both[256:512]
            total = total + jnp.sum(mixed * cells.astype(F32), axis=0, keepdims=True)
            send4[s, :, u] = mixed.astype(BF16).reshape(16, 16, 128)
        redsend[s, 1:2, :] = total

        def one(step, carry):
            peer = z_peer(step)
            pltpu.make_async_remote_copy(
                src_ref=redsend.at[s], dst_ref=redz.at[s, mz],
                send_sem=send_sem.at[6, s], recv_sem=recv_sem.at[6, s],
                device_id={"tm": peer}, device_id_type=MESH,
            ).start()
            return carry

        lax.fori_loop(0, ZN - 1, one, 0)
        redz[s, mz] = redsend[s]
        start_z(4, s, send4, recv4)

    def sums_lon(s):
        whole_z(6, s, redz, redz).wait_recv()
        redmid[s] = jnp.sum(redz[s], axis=0)

        def one(step, carry):
            pltpu.make_async_remote_copy(
                src_ref=redmid.at[s], dst_ref=redl.at[s, ml],
                send_sem=send_sem.at[7, s], recv_sem=recv_sem.at[7, s],
                device_id={"lon": l_peer(step)}, device_id_type=MESH,
            ).start()
            return carry

        lax.fori_loop(0, LN - 1, one, 0)
        redl[s, ml] = redmid[s]

    def sums_whole(s):
        part = redl.at[s, pl.ds(0, LN - 1)]
        return pltpu.make_async_remote_copy(
            src_ref=part, dst_ref=part, send_sem=send_sem.at[7, s], recv_sem=recv_sem.at[7, s],
            device_id={"lon": l_peer(0)}, device_id_type=MESH,
        )

    def lat_last(s):
        whole_z(4, s, send4, recv4).wait_recv()

        def widen(i, carry):
            ssc[pl.ds(pl.multiple_of(i * 64, 64), 64), :] = recv4[s, i].reshape(64, 128).astype(F32)
            return carry

        lax.fori_loop(0, ZN, widen, 0)

        def turn(u, carry):
            parts = [ssc[pl.ds(u * 16 + h, 16, stride=64), :] for h in range(16)]
            parts = exchange(parts, (8, 16, 32, 64))
            for bb in range(16):
                xd[0, pl.ds(bb * 16, 16), columns(u, 128)] = parts[bb].astype(BF16)
            return carry

        lax.fori_loop(0, 4, turn, 0)
        for n in range(2):
            cols = slice(n * 256, (n + 1) * 256)
            ysc[:, cols] = dot(latq[...], xd[0, :, cols], NN)
        to_lon(s, send5)
        start_l(5, s, send5, recv5)

    def lon_last(s):
        sums_whole(s).wait_recv()
        total = jnp.sum(redl[s], axis=0)
        norm_sq = jnp.sum(total[0:1], axis=1, keepdims=True)
        quad = jnp.sum(total[1:2], axis=1, keepdims=True)
        step_size = norm_sq / (quad + NOISE_VAR * norm_sq)
        whole_l(5, s, send5, recv5).wait_recv()
        lon_columns(s, recv5)

        def block(n, carry):
            both = dot(halves[...], lonfull[columns(n, 256), :], NT)
            applied = both[0:128] + both[128:256]
            left = resid[s, :, columns(n, 256)]
            operated = mask[:, columns(n, 256)].astype(F32) * applied + NOISE_VAR * left
            post[s, :, columns(n, 256)] = prior[s, :, columns(n, 256)] + step_size * applied
            nxt[s, :, columns(n, 256)] = left - step_size * operated
            return carry

        lax.fori_loop(0, 4, block, 0)

    lat_first(0)
    gathered.wait_recv()
    lon_first(0)
    lat_first(1)
    lat_back(0)
    lon_first(1)
    lat_back(1)
    hours_mix(0)
    hours_mix(1)
    sums_lon(0)
    sums_lon(1)
    lat_last(0)
    lon_last(0)
    lat_last(1)
    lon_last(1)

    gathered.wait_send()
    for s in range(2):
        whole_z(0, s, send0, recv0).wait_send()
        whole_l(1, s, send1, recv1).wait_send()
        whole_l(2, s, send2, recv2).wait_send()
        whole_z(3, s, send3, recv3).wait_send()
        whole_z(4, s, send4, recv4).wait_send()
        whole_l(5, s, send5, recv5).wait_send()
        whole_z(6, s, redz, redz).wait_send()
        sums_whole(s).wait_send()


def trig(step, period, count, columns):
    angle = 2.0 * np.pi * ((step * np.arange(count)[:, None] * np.arange(columns)[None]) % period) / period
    return np.concatenate([np.cos(angle), np.sin(angle)]).astype(np.float32)


def shards(noise, observed, mask, lat_factor, lon_factor, spectrum):
    periods = noise.shape[3]
    powers = jnp.concatenate([spectrum, spectrum[1:-1][::-1]])
    amplitude = jnp.sqrt(powers / periods)[None]
    coarse = jnp.asarray(trig(16, 512, 16, 512))
    fine = jnp.asarray(trig(1, 512, 16, 512))
    vmem = pl.BlockSpec(memory_space=pltpu.VMEM)
    anywhere = pl.BlockSpec(memory_space=pl.ANY)
    zbuf = pltpu.VMEM((2, 16, 4, 16, 128), BF16)
    lbuf = pltpu.VMEM((2, 1024, 128), F32)
    scratch = [
        pltpu.VMEM((128, 1024), F32),
        pltpu.VMEM((128, 1024), jnp.int32),
        pltpu.VMEM((2, 2, 128, 1024), BF16),
        pltpu.VMEM((2, 256, 1024), BF16),
        pltpu.VMEM((512, 128), F32),
        pltpu.VMEM((256, 512), F32),
        pltpu.VMEM((1024, 128), F32),
        pltpu.VMEM((512, 128), F32),
        pltpu.VMEM((256, 256), BF16),
        pltpu.VMEM((256, 256), BF16),
        pltpu.VMEM((256, 256), BF16),
        pltpu.VMEM((512, 256), BF16),
        pltpu.VMEM((1024, 1024), BF16),
        pltpu.VMEM((256, 1024), BF16),
        pltpu.VMEM((2, 256, 512), BF16),
        pltpu.VMEM((2, 128, 1024), F32),
        pltpu.VMEM((2, 128, 1024), F32),
        zbuf, zbuf, lbuf, lbuf, lbuf, lbuf, zbuf, zbuf, zbuf, zbuf, lbuf, lbuf,
        pltpu.VMEM((2, 8, 128), F32),
        pltpu.VMEM((2, 16, 8, 128), F32),
        pltpu.VMEM((2, 8, 128), F32),
        pltpu.VMEM((2, 32, 8, 128), F32),
        pltpu.SemaphoreType.DMA((HOPS, 2)),
        pltpu.SemaphoreType.DMA((HOPS, 2)),
        pltpu.SemaphoreType.DMA((4,)),
    ]
    out = jax.ShapeDtypeStruct((2, 128, 1024), F32)
    post, nxt = pl.pallas_call(
        body,
        out_shape=(out, out),
        in_specs=[vmem, anywhere, anywhere, vmem, vmem, vmem, vmem, vmem],
        out_specs=(vmem, vmem),
        scratch_shapes=scratch,
        compiler_params=pltpu.CompilerParams(
            collective_id=0, has_side_effects=True, vmem_limit_bytes=50 << 20
        ),
        name="posterior",
    )(
        noise, observed.reshape(128, 1024), mask.reshape(128, 1024), lat_factor, lon_factor, amplitude, coarse, fine
    )
    return post.reshape(2, 16, 8, 1024), nxt.reshape(2, 16, 8, 1024)


def solution(mesh):
    return jax.shard_map(
        shards,
        mesh=mesh,
        in_specs=(
            P(None, "tm", "lon", None),
            P("tm", "lon", None),
            P("tm", "lon", None),
            P(),
            P("lon", None),
            P(),
        ),
        out_specs=(P(None, "tm", "lon", None), P(None, "tm", "lon", None)),
        check_vma=False,
    )
```

```python
import functools

import jax
import jax.numpy as jnp
import numpy as np
from jax import lax
from jax.experimental import pallas as pl
from jax.experimental.pallas import tpu as pltpu
from jax.sharding import PartitionSpec as P

F32 = jnp.float32
BF16 = jnp.bfloat16
MESH = pl.DeviceIdType.MESH
NOISE_VAR = 0.25
NT = (((1,), (1,)), ((), ()))
NN = (((1,), (0,)), ((), ()))
HOPS = 8
ZN = 16
LN = 32


def repeat(count, step):
    lax.fori_loop(0, count, step, 0, unroll=min(count, 8))


def dot(left, right, dims):
    return lax.dot_general(left, right, dims, preferred_element_type=F32)


def split(value):
    high = value.astype(BF16)
    return high, (value - high.astype(F32)).astype(BF16)


def exchange(parts, strides):
    parts = list(parts)
    lane = lax.broadcasted_iota(jnp.int32, parts[0].shape, 1)
    for bit, stride in enumerate(strides):
        low_lanes = (lane & stride) == 0
        for first in range(len(parts)):
            if first & (1 << bit):
                continue
            second = first | (1 << bit)
            low, high = parts[first], parts[second]
            parts[first] = jnp.where(low_lanes, low, pltpu.roll(high, stride, 1))
            parts[second] = jnp.where(low_lanes, pltpu.roll(low, 128 - stride, 1), high)
    return parts


def body(
    noise_hbm, obs_hbm, mask_hbm, lat_hbm, lon_hbm, amp, coarse_hbm, fine_hbm,
    post, nxt,
    noise, lat, lon, coarse, fine, obs, mask, tab, waves, work, ysc, ssc, lat32, latp, latq, latqt, hour,
    lonfull, halves, xd, prior, resid,
    send0, recv0, send1, recv1, send2, recv2, send3, recv3, send4, recv4, send5, recv5,
    redsend, redz, redmid, redl,
    send_sem, recv_sem, local_sem,
):
    mz = lax.axis_index("tm")
    ml = lax.axis_index("lon")

    def z_peer(step):
        away = (step // 2 + 1) * (1 - 2 * (step % 2))
        return lax.rem(mz + away + ZN, ZN)

    def l_peer(step):
        return lax.rem(ml + step + 1, LN)

    fetches = [
        pltpu.make_async_copy(src, dst, local_sem.at[index])
        for index, (src, dst) in enumerate(
            [(coarse_hbm, coarse), (fine_hbm, fine), (noise_hbm, noise), (lat_hbm, lat), (lon_hbm, lon),
             (obs_hbm, obs), (mask_hbm, mask)]
        )
    ]
    for fetch in fetches:
        fetch.start()
    barrier = pltpu.get_barrier_semaphore()

    def greet_z(step, carry):
        pl.semaphore_signal(barrier, inc=1, device_id={"tm": z_peer(step)}, device_id_type=MESH)
        return carry

    def greet_l(step, carry):
        pl.semaphore_signal(barrier, inc=1, device_id={"lon": l_peer(step)}, device_id_type=MESH)
        return carry

    lax.fori_loop(0, ZN - 1, greet_z, 0)
    lax.fori_loop(0, LN - 1, greet_l, 0)

    def start_z(hop, s, src, dst):
        def one(step, carry):
            peer = z_peer(step)
            pltpu.make_async_remote_copy(
                src_ref=src.at[s, peer], dst_ref=dst.at[s, mz],
                send_sem=send_sem.at[hop, s], recv_sem=recv_sem.at[hop, s],
                device_id={"tm": peer}, device_id_type=MESH,
            ).start()
            return carry

        lax.fori_loop(0, ZN - 1, one, 0)
        dst[s, mz] = src[s, mz]

    def whole_z(hop, s, src, dst):
        return pltpu.make_async_remote_copy(
            src_ref=src.at[s, pl.ds(0, ZN - 1)], dst_ref=dst.at[s, pl.ds(0, ZN - 1)],
            send_sem=send_sem.at[hop, s], recv_sem=recv_sem.at[hop, s],
            device_id={"tm": z_peer(0)}, device_id_type=MESH,
        )

    def start_l(hop, s, src, dst):
        def one(step, carry):
            peer = l_peer(step)
            pltpu.make_async_remote_copy(
                src_ref=src.at[s, pl.ds(pl.multiple_of(peer * 32, 32), 32)],
                dst_ref=dst.at[s, pl.ds(pl.multiple_of(ml * 32, 32), 32)],
                send_sem=send_sem.at[hop, s], recv_sem=recv_sem.at[hop, s],
                device_id={"lon": peer}, device_id_type=MESH,
            ).start()
            return carry

        lax.fori_loop(0, LN - 1, one, 0)
        own = pl.ds(pl.multiple_of(ml * 32, 32), 32)
        dst[s, own] = src[s, own]

    def whole_l(hop, s, src, dst):
        rows = pl.ds(0, (LN - 1) * 32)
        return pltpu.make_async_remote_copy(
            src_ref=src.at[s, rows], dst_ref=dst.at[s, rows],
            send_sem=send_sem.at[hop, s], recv_sem=recv_sem.at[hop, s],
            device_id={"lon": l_peer(0)}, device_id_type=MESH,
        )

    for fetch in fetches[:5]:
        fetch.wait()
    amp_row = amp[...]

    def tables(group):
        base = pl.multiple_of(group * 8, 8)
        c1 = coarse[pl.ds(base, 8), :]
        s1 = coarse[pl.ds(16 + base, 8), :]
        for pair in range(8):
            cos_rows, sin_rows = [], []
            for hh in (2 * pair, 2 * pair + 1):
                c2, s2 = fine[hh : hh + 1, :], fine[16 + hh : 17 + hh, :]
                cos_rows.append((c1 * c2 - s1 * s2) * amp_row)
                sin_rows.append((s1 * c2 + c1 * s2) * amp_row)
            cw = jnp.concatenate(cos_rows, axis=0).astype(BF16)
            sw = jnp.concatenate(sin_rows, axis=0).astype(BF16)
            rows = pl.ds(pair * 16, 16)
            tab[0, group, rows, 0:512] = cw
            tab[0, group, rows, 512:1024] = sw
            tab[1, group, rows, 0:512] = -sw
            tab[1, group, rows, 512:1024] = cw

    def tables_loop(group, carry):
        tables(group)
        return carry

    lax.fori_loop(0, 2, tables_loop, 0)

    def transform(s):
        def one(group, carry):
            for part in range(2):
                rows = noise[part].reshape(512, 512)
                term = dot(rows, tab[s, group, :, part * 512 : (part + 1) * 512], NT)
                if part == 0:
                    work[0:512, :] = term
                else:
                    work[0:512, :] += term

            def swap(u, inner):
                parts = [work[pl.ds(u * 8 + og, 16, stride=32), :] for og in range(8)]
                parts = exchange(parts, (1, 2, 4))
                for jl in range(8):
                    send0[s, group * 8 + jl, u] = parts[jl].astype(BF16)
                return inner

            repeat(4, swap)
            return carry

        lax.fori_loop(0, 2, one, 0)

    transform(0)
    transform(1)

    def spread(value):
        lat32[0:256, :] = value[:, 0:128]
        lat32[256:512, :] = value[:, 128:256]

    spread(lat[...].astype(F32))
    for k in range(8):
        latp[k * 32 : (k + 1) * 32, :] = jnp.concatenate(
            [lat32[pl.ds(c * 256 + k, 32, stride=8), :] for c in range(2)], axis=1
        ).astype(BF16)
    spread(latp[...].astype(F32).T)
    for bb in range(16):
        latqt[bb * 16 : (bb + 1) * 16, :] = jnp.concatenate(
            [lat32[pl.ds(c * 256 + bb, 16, stride=16), :] for c in range(2)], axis=1
        ).astype(BF16)
    latq[...] = latqt[...].astype(F32).T.astype(BF16)

    def wave(j, carry):
        c1 = coarse[pl.ds(j, 1), :] * amp_row
        s1 = coarse[pl.ds(16 + j, 1), :] * amp_row
        c2, s2 = fine[0:16, :], fine[16:32, :]
        rows = pl.ds(pl.multiple_of(j * 16, 16), 16)
        for part, value in enumerate((c1 * c2 - s1 * s2, s1 * c2 + c1 * s2)):
            high, low = split(value)
            waves[0, rows, part * 512 : (part + 1) * 512] = high
            waves[1, rows, part * 512 : (part + 1) * 512] = low
        return carry

    lax.fori_loop(0, ZN, wave, 0)
    cross = dot(waves[0], waves[1], NT)
    kernel = dot(waves[0], waves[0], NT) + (cross + cross.T)
    high, low = split(kernel)
    hour[0:256, :] = high
    hour[256:512, :] = low
    redsend[...] = jnp.zeros_like(redsend)
    fetches[5].wait()
    fetches[6].wait()

    pl.semaphore_wait(barrier, ZN + LN - 2)
    start_z(0, 0, send0, recv0)

    own_rows = pl.ds(pl.multiple_of(ml * 32, 32), 32)

    def gather(step, carry):
        pltpu.make_async_remote_copy(
            src_ref=lon, dst_ref=lonfull.at[own_rows],
            send_sem=local_sem.at[7], recv_sem=local_sem.at[8],
            device_id={"lon": l_peer(step)}, device_id_type=MESH,
        ).start()
        return carry

    lax.fori_loop(0, LN - 1, gather, 0)
    lonfull[own_rows, :] = lon[...]
    gathered = pltpu.make_async_remote_copy(
        src_ref=lonfull.at[pl.ds(0, 31 * 32)], dst_ref=lonfull.at[pl.ds(0, 31 * 32)],
        send_sem=local_sem.at[7], recv_sem=local_sem.at[8],
        device_id={"lon": l_peer(0)}, device_id_type=MESH,
    )
    def columns(index, width):
        return pl.ds(pl.multiple_of(index * width, width), width)

    def to_lon(s, dst):
        def swap(step, carry):
            u, lb = step // 2, step % 2
            parts = [
                ysc[pl.ds(pl.multiple_of(k * 32 + lb * 16, 16), 16), columns(u, 128)] for k in range(8)
            ]
            parts = exchange(parts, (1, 2, 4))
            for og in range(8):
                ssc[pl.ds(pl.multiple_of((u * 8 + og) * 32 + lb * 16, 16), 16), :] = parts[og]
            return carry

        repeat(8, swap)

        def pick(peer, carry):
            dst[s, pl.ds(pl.multiple_of(peer * 32, 32), 32), :] = ssc[pl.ds(peer, 32, stride=32), :]
            return carry

        repeat(LN, pick)

    def lat_first(s):
        whole_z(0, s, send0, recv0).wait_recv()
        if s == 0:
            start_z(0, 1, send0, recv0)
        for u in range(4):
            ysc[:, u * 128 : (u + 1) * 128] = dot(latp[...], recv0[s, :, u].reshape(256, 128), NN)
        to_lon(s, send1)
        start_l(1, s, send1, recv1)

    def lon_columns(s, src):
        def turn(c, carry):
            block = src[s, columns(c, 128), :].T
            high, low = split(block)
            halves[0:128, columns(c, 128)] = high
            halves[128:256, columns(c, 128)] = low
            return carry

        repeat(8, turn)

    def lon_first(s):
        whole_l(1, s, send1, recv1).wait_recv()
        lon_columns(s, recv1)

        def prior_block(n, total):
            both = dot(halves[...], lonfull[columns(n, 256), :], NT)
            drawn = both[0:128] + both[128:256]
            left = mask[:, columns(n, 256)].astype(F32) * (obs[:, columns(n, 256)] - drawn)
            prior[s, :, columns(n, 256)] = drawn
            resid[s, :, columns(n, 256)] = left
            squares = jnp.sum(left * left, axis=0, keepdims=True)
            return total + squares[:, 0:128] + squares[:, 128:256]

        redsend[s, 0:1, :] = lax.fori_loop(0, 4, prior_block, jnp.zeros((1, 128), F32))

        def halve(n, carry):
            high, low = split(resid[s, :, columns(n, 256)])
            halves[0:128, columns(n, 256)] = high
            halves[128:256, columns(n, 256)] = low
            return carry

        repeat(4, halve)

        def back_block(n, carry):
            both = dot(halves[...], lonfull[:, columns(n, 256)], NN)
            summed = both[0:128] + both[128:256]
            for part in range(2):
                rows = pl.ds(pl.multiple_of(n * 256 + part * 128, 128), 128)
                send2[s, rows, :] = summed[:, part * 128 : (part + 1) * 128].T.astype(BF16)
            return carry

        repeat(4, back_block)
        start_l(2, s, send2, recv2)

    def lat_back(s):
        whole_l(2, s, send2, recv2).wait_recv()
        ssc[...] = recv2[s].astype(F32)

        def swap(step, carry):
            u, lb = step // 2, step % 2
            parts = [ssc[pl.ds(lb * 512 + u * 8 + pg, 16, stride=32), :] for pg in range(8)]
            parts = exchange(parts, (1, 2, 4))
            for k in range(8):
                rows = pl.ds(pl.multiple_of(k * 32 + lb * 16, 16), 16)
                xd[rows, columns(u, 128)] = parts[k].astype(BF16)
            return carry

        repeat(8, swap)
        for n in range(2):
            cols = slice(n * 256, (n + 1) * 256)
            ysc[:, cols] = dot(latqt[...], xd[:, cols], NN)

        def turn(step, carry):
            u, ib = step // 2, step % 2
            parts = [ysc[pl.ds(pl.multiple_of(bb * 16 + ib * 8, 8), 8), columns(u, 128)] for bb in range(16)]
            parts = exchange(parts, (8, 16, 32, 64))
            for h in range(16):
                ssc[pl.ds(pl.multiple_of((u * 16 + h) * 16 + ib * 8, 8), 8), :] = parts[h]
            return carry

        repeat(8, turn)

        def pick(peer, carry):
            for u in range(4):
                send3[s, peer, u] = ssc[pl.ds(u * 256 + peer, 16, stride=16), :].astype(BF16)
            return carry

        repeat(ZN, pick)
        start_z(3, s, send3, recv3)

    def hours_mix(s):
        whole_z(3, s, send3, recv3).wait_recv()
        total = jnp.zeros((1, 128), F32)
        for u in range(4):
            cells = recv3[s, :, u].reshape(256, 128)
            both = dot(hour[...], cells, NN)
            mixed = both[0:256] + both[256:512]
            total = total + jnp.sum(mixed * cells.astype(F32), axis=0, keepdims=True)
            send4[s, :, u] = mixed.astype(BF16).reshape(16, 16, 128)
        redsend[s, 1:2, :] = total

        def one(step, carry):
            peer = z_peer(step)
            pltpu.make_async_remote_copy(
                src_ref=redsend.at[s], dst_ref=redz.at[s, mz],
                send_sem=send_sem.at[6, s], recv_sem=recv_sem.at[6, s],
                device_id={"tm": peer}, device_id_type=MESH,
            ).start()
            return carry

        lax.fori_loop(0, ZN - 1, one, 0)
        redz[s, mz] = redsend[s]
        start_z(4, s, send4, recv4)

    def sums_lon(s):
        whole_z(6, s, redz, redz).wait_recv()
        redmid[s] = jnp.sum(redz[s], axis=0)

        def one(step, carry):
            pltpu.make_async_remote_copy(
                src_ref=redmid.at[s], dst_ref=redl.at[s, ml],
                send_sem=send_sem.at[7, s], recv_sem=recv_sem.at[7, s],
                device_id={"lon": l_peer(step)}, device_id_type=MESH,
            ).start()
            return carry

        lax.fori_loop(0, LN - 1, one, 0)
        redl[s, ml] = redmid[s]

    def sums_whole(s):
        part = redl.at[s, pl.ds(0, LN - 1)]
        return pltpu.make_async_remote_copy(
            src_ref=part, dst_ref=part, send_sem=send_sem.at[7, s], recv_sem=recv_sem.at[7, s],
            device_id={"lon": l_peer(0)}, device_id_type=MESH,
        )

    def lat_last(s):
        whole_z(4, s, send4, recv4).wait_recv()

        def widen(i, carry):
            ssc[pl.ds(pl.multiple_of(i * 64, 64), 64), :] = recv4[s, i].reshape(64, 128).astype(F32)
            return carry

        repeat(ZN, widen)

        def turn(u, carry):
            parts = [ssc[pl.ds(u * 16 + h, 16, stride=64), :] for h in range(16)]
            parts = exchange(parts, (8, 16, 32, 64))
            for bb in range(16):
                xd[pl.ds(bb * 16, 16), columns(u, 128)] = parts[bb].astype(BF16)
            return carry

        repeat(4, turn)
        for n in range(2):
            cols = slice(n * 256, (n + 1) * 256)
            ysc[:, cols] = dot(latq[...], xd[:, cols], NN)
        to_lon(s, send5)
        start_l(5, s, send5, recv5)

    def lon_last(s):
        sums_whole(s).wait_recv()
        total = jnp.sum(redl[s], axis=0)
        norm_sq = jnp.sum(total[0:1], axis=1, keepdims=True)
        quad = jnp.sum(total[1:2], axis=1, keepdims=True)
        step_size = norm_sq / (quad + NOISE_VAR * norm_sq)
        whole_l(5, s, send5, recv5).wait_recv()
        lon_columns(s, recv5)

        def block(n, carry):
            both = dot(halves[...], lonfull[columns(n, 256), :], NT)
            applied = both[0:128] + both[128:256]
            left = resid[s, :, columns(n, 256)]
            operated = mask[:, columns(n, 256)].astype(F32) * applied + NOISE_VAR * left
            post[s, :, columns(n, 256)] = prior[s, :, columns(n, 256)] + step_size * applied
            nxt[s, :, columns(n, 256)] = left - step_size * operated
            return carry

        repeat(4, block)

    lat_first(0)
    gathered.wait_recv()
    lon_first(0)
    lat_first(1)
    lat_back(0)
    lon_first(1)
    lat_back(1)
    hours_mix(0)
    hours_mix(1)
    sums_lon(0)
    sums_lon(1)
    lat_last(0)
    lon_last(0)
    lat_last(1)
    lon_last(1)

    gathered.wait_send()
    for s in range(2):
        whole_z(0, s, send0, recv0).wait_send()
        whole_l(1, s, send1, recv1).wait_send()
        whole_l(2, s, send2, recv2).wait_send()
        whole_z(3, s, send3, recv3).wait_send()
        whole_z(4, s, send4, recv4).wait_send()
        whole_l(5, s, send5, recv5).wait_send()
        whole_z(6, s, redz, redz).wait_send()
        sums_whole(s).wait_send()


def trig(step, period, count, columns):
    angle = 2.0 * np.pi * ((step * np.arange(count)[:, None] * np.arange(columns)[None]) % period) / period
    return np.concatenate([np.cos(angle), np.sin(angle)]).astype(np.float32)


def shards(noise, observed, mask, lat_factor, lon_factor, spectrum):
    periods = noise.shape[3]
    powers = jnp.concatenate([spectrum, spectrum[1:-1][::-1]])
    amplitude = jnp.sqrt(powers / periods)[None]
    coarse = jnp.asarray(trig(16, 512, 16, 512))
    fine = jnp.asarray(trig(1, 512, 16, 512))
    vmem = pl.BlockSpec(memory_space=pltpu.VMEM)
    hbm = pl.BlockSpec(memory_space=pltpu.HBM)
    zbuf = pltpu.VMEM((2, 16, 4, 16, 128), BF16)
    lbuf = pltpu.VMEM((2, 1024, 128), F32)
    lhalf = pltpu.VMEM((2, 1024, 128), BF16)
    scratch = [
        pltpu.VMEM((2, 16, 32, 512), BF16),
        pltpu.VMEM((256, 256), BF16),
        pltpu.VMEM((32, 1024), BF16),
        pltpu.VMEM((32, 512), F32),
        pltpu.VMEM((32, 512), F32),
        pltpu.VMEM((128, 1024), F32),
        pltpu.VMEM((128, 1024), jnp.int32),
        pltpu.VMEM((2, 2, 128, 1024), BF16),
        pltpu.VMEM((2, 256, 1024), BF16),
        pltpu.VMEM((512, 128), F32),
        pltpu.VMEM((256, 512), F32),
        pltpu.VMEM((1024, 128), F32),
        pltpu.VMEM((512, 128), F32),
        pltpu.VMEM((256, 256), BF16),
        pltpu.VMEM((256, 256), BF16),
        pltpu.VMEM((256, 256), BF16),
        pltpu.VMEM((512, 256), BF16),
        pltpu.VMEM((1024, 1024), BF16),
        pltpu.VMEM((256, 1024), BF16),
        pltpu.VMEM((256, 512), BF16),
        pltpu.VMEM((2, 128, 1024), F32),
        pltpu.VMEM((2, 128, 1024), F32),
        zbuf, zbuf, lbuf, lbuf, lhalf, lhalf, zbuf, zbuf, zbuf, zbuf, lbuf, lbuf,
        pltpu.VMEM((2, 8, 128), F32),
        pltpu.VMEM((2, 16, 8, 128), F32),
        pltpu.VMEM((2, 8, 128), F32),
        pltpu.VMEM((2, 32, 8, 128), F32),
        pltpu.SemaphoreType.DMA((HOPS, 2)),
        pltpu.SemaphoreType.DMA((HOPS, 2)),
        pltpu.SemaphoreType.DMA((9,)),
    ]
    out = jax.ShapeDtypeStruct((2, 128, 1024), F32)
    post, nxt = pl.pallas_call(
        body,
        out_shape=(out, out),
        in_specs=[hbm] * 5 + [vmem] + [hbm] * 2,
        out_specs=(vmem, vmem),
        scratch_shapes=scratch,
        compiler_params=pltpu.CompilerParams(
            collective_id=0, has_side_effects=True, vmem_limit_bytes=44 << 20
        ),
        name="posterior",
    )(
        noise, observed.reshape(128, 1024), mask.reshape(128, 1024), lat_factor, lon_factor, amplitude, coarse, fine
    )
    return post.reshape(2, 16, 8, 1024), nxt.reshape(2, 16, 8, 1024)


def solution(mesh):
    return jax.shard_map(
        shards,
        mesh=mesh,
        in_specs=(
            P(None, "tm", "lon", None),
            P("tm", "lon", None),
            P("tm", "lon", None),
            P(),
            P("lon", None),
            P(),
        ),
        out_specs=(P(None, "tm", "lon", None), P(None, "tm", "lon", None)),
        check_vma=False,
    )
```

```python
import functools

import jax
import jax.numpy as jnp
import numpy as np
from jax import lax
from jax.experimental import pallas as pl
from jax.experimental.pallas import tpu as pltpu
from jax.sharding import PartitionSpec as P

F32 = jnp.float32
BF16 = jnp.bfloat16
MESH = pl.DeviceIdType.MESH
NOISE_VAR = 0.25
NT = (((1,), (1,)), ((), ()))
NN = (((1,), (0,)), ((), ()))
HOPS = 8
ZN = 16
LN = 32


def repeat(count, step):
    lax.fori_loop(0, count, step, 0, unroll=min(count, 8))


def dot(left, right, dims):
    return lax.dot_general(left, right, dims, preferred_element_type=F32)


def split(value):
    high = value.astype(BF16)
    return high, (value - high.astype(F32)).astype(BF16)


def exchange(parts, strides):
    parts = list(parts)
    lane = lax.broadcasted_iota(jnp.int32, parts[0].shape, 1)
    for bit, stride in enumerate(strides):
        low_lanes = (lane & stride) == 0
        for first in range(len(parts)):
            if first & (1 << bit):
                continue
            second = first | (1 << bit)
            low, high = parts[first], parts[second]
            parts[first] = jnp.where(low_lanes, low, pltpu.roll(high, stride, 1))
            parts[second] = jnp.where(low_lanes, pltpu.roll(low, 128 - stride, 1), high)
    return parts


def body(
    noise_hbm, obs_hbm, mask_hbm, lat_hbm, lon_hbm, amp, coarse_hbm, fine_hbm,
    post, nxt,
    noise, lat, lon, coarse, fine, obs, mask, tab, waves, work, ysc, ssc, lat32, latp, latq, latqt, hour,
    lonfull, halves, xd, prior, resid,
    send0, recv0, send1, recv1, send2, recv2, send3, recv3, send4, recv4, send5, recv5,
    redsend, redz, redmid, redl,
    send_sem, recv_sem, gather_send, gather_recv, local_sem,
):
    mz = lax.axis_index("tm")
    ml = lax.axis_index("lon")

    def z_peer(step):
        away = (8 - (step + 1) // 2) * (1 - 2 * (step % 2))
        return lax.rem(mz + away + ZN, ZN)

    def l_peer(step):
        return lax.rem(ml + step + 1, LN)

    fetches = [
        pltpu.make_async_copy(src, dst, local_sem.at[index])
        for index, (src, dst) in enumerate(
            [(coarse_hbm, coarse), (fine_hbm, fine), (noise_hbm, noise), (lat_hbm, lat), (lon_hbm, lon),
             (obs_hbm, obs), (mask_hbm, mask)]
        )
    ]
    for fetch in fetches:
        fetch.start()
    barrier = pltpu.get_barrier_semaphore()

    def greet_z(step, carry):
        pl.semaphore_signal(barrier, inc=1, device_id={"tm": z_peer(step)}, device_id_type=MESH)
        return carry

    def greet_l(step, carry):
        pl.semaphore_signal(barrier, inc=1, device_id={"lon": l_peer(step)}, device_id_type=MESH)
        return carry

    lax.fori_loop(0, ZN - 1, greet_z, 0)
    lax.fori_loop(0, LN - 1, greet_l, 0)

    def send_z(hop, s, src, dst, peer):
        pltpu.make_async_remote_copy(
            src_ref=src.at[s, peer], dst_ref=dst.at[s, mz],
            send_sem=send_sem.at[hop, s], recv_sem=recv_sem.at[hop, s],
            device_id={"tm": peer}, device_id_type=MESH,
        ).start()

    def start_z(hop, s, src, dst):
        def one(step, carry):
            send_z(hop, s, src, dst, z_peer(step))
            return carry

        lax.fori_loop(0, ZN - 1, one, 0)
        dst[s, mz] = src[s, mz]

    def whole_z(hop, s, src, dst):
        return pltpu.make_async_remote_copy(
            src_ref=src.at[s, pl.ds(0, ZN - 1)], dst_ref=dst.at[s, pl.ds(0, ZN - 1)],
            send_sem=send_sem.at[hop, s], recv_sem=recv_sem.at[hop, s],
            device_id={"tm": z_peer(0)}, device_id_type=MESH,
        )

    def peer_rows(peer):
        return pl.ds(pl.multiple_of(peer * 32, 32), 32)

    def send_l(hop, s, src, dst, peer):
        pltpu.make_async_remote_copy(
            src_ref=src.at[s, peer_rows(peer)], dst_ref=dst.at[s, peer_rows(ml)],
            send_sem=send_sem.at[hop, s], recv_sem=recv_sem.at[hop, s],
            device_id={"lon": peer}, device_id_type=MESH,
        ).start()

    def whole_l(hop, s, src, dst):
        rows = pl.ds(0, (LN - 1) * 32)
        return pltpu.make_async_remote_copy(
            src_ref=src.at[s, rows], dst_ref=dst.at[s, rows],
            send_sem=send_sem.at[hop, s], recv_sem=recv_sem.at[hop, s],
            device_id={"lon": l_peer(0)}, device_id_type=MESH,
        )

    for fetch in fetches[:5]:
        fetch.wait()
    amp_row = amp[...]

    def tables(group):
        base = pl.multiple_of(group * 8, 8)
        c1 = coarse[pl.ds(base, 8), :]
        s1 = coarse[pl.ds(16 + base, 8), :]
        for pair in range(8):
            cos_rows, sin_rows = [], []
            for hh in (2 * pair, 2 * pair + 1):
                c2, s2 = fine[hh : hh + 1, :], fine[16 + hh : 17 + hh, :]
                cos_rows.append((c1 * c2 - s1 * s2) * amp_row)
                sin_rows.append((s1 * c2 + c1 * s2) * amp_row)
            cw = jnp.concatenate(cos_rows, axis=0).astype(BF16)
            sw = jnp.concatenate(sin_rows, axis=0).astype(BF16)
            rows = pl.ds(pair * 16, 16)
            tab[0, group, rows, 0:512] = cw
            tab[0, group, rows, 512:1024] = sw
            tab[1, group, rows, 0:512] = -sw
            tab[1, group, rows, 512:1024] = cw

    def tables_loop(group, carry):
        tables(group)
        return carry

    lax.fori_loop(0, 2, tables_loop, 0)

    def transform(s):
        def one(group, carry):
            for part in range(2):
                rows = noise[part].reshape(512, 512)
                term = dot(rows, tab[s, group, :, part * 512 : (part + 1) * 512], NT)
                if part == 0:
                    work[0:512, :] = term
                else:
                    work[0:512, :] += term

            def swap(u, inner):
                parts = [work[pl.ds(u * 8 + og, 16, stride=32), :] for og in range(8)]
                parts = exchange(parts, (1, 2, 4))
                for jl in range(8):
                    send0[s, group * 8 + jl, u] = parts[jl].astype(BF16)
                return inner

            repeat(4, swap)
            return carry

        lax.fori_loop(0, 2, one, 0)

    transform(0)
    transform(1)

    def spread(value):
        lat32[0:256, :] = value[:, 0:128]
        lat32[256:512, :] = value[:, 128:256]

    spread(lat[...].astype(F32))
    for k in range(8):
        latp[k * 32 : (k + 1) * 32, :] = jnp.concatenate(
            [lat32[pl.ds(c * 256 + k, 32, stride=8), :] for c in range(2)], axis=1
        ).astype(BF16)
    spread(latp[...].astype(F32).T)
    for bb in range(16):
        latqt[bb * 16 : (bb + 1) * 16, :] = jnp.concatenate(
            [lat32[pl.ds(c * 256 + bb, 16, stride=16), :] for c in range(2)], axis=1
        ).astype(BF16)
    latq[...] = latqt[...].astype(F32).T.astype(BF16)

    def wave(j, carry):
        c1 = coarse[pl.ds(j, 1), :] * amp_row
        s1 = coarse[pl.ds(16 + j, 1), :] * amp_row
        c2, s2 = fine[0:16, :], fine[16:32, :]
        rows = pl.ds(pl.multiple_of(j * 16, 16), 16)
        for part, value in enumerate((c1 * c2 - s1 * s2, s1 * c2 + c1 * s2)):
            high, low = split(value)
            waves[0, rows, part * 512 : (part + 1) * 512] = high
            waves[1, rows, part * 512 : (part + 1) * 512] = low
        return carry

    lax.fori_loop(0, ZN, wave, 0)
    cross = dot(waves[0], waves[1], NT)
    kernel = dot(waves[0], waves[0], NT) + (cross + cross.T)
    high, low = split(kernel)
    hour[0:256, :] = high
    hour[256:512, :] = low
    redsend[...] = jnp.zeros_like(redsend)
    fetches[5].wait()
    fetches[6].wait()

    lonfull[peer_rows(ml), :] = lon[...]
    for kind in range(3):
        rest = 1024 - 256 * (kind + 1)
        lonfull[256 * kind : 256 * (kind + 1), 1024 - rest :] = jnp.zeros((256, rest), BF16)
    pl.semaphore_wait(barrier, ZN + LN - 2)
    start_z(0, 0, send0, recv0)

    sibling = ml + 1 - 2 * lax.rem(ml, 2)
    own_class = ml // 8

    def gather_copy(kind, rows, peer, cross):
        width = 256 * (kind + 1)
        return pltpu.make_async_remote_copy(
            src_ref=lonfull.at[rows, pl.ds(0, width)], dst_ref=lonfull.at[rows, pl.ds(0, width)],
            send_sem=gather_send.at[cross, kind], recv_sem=gather_recv.at[cross, kind],
            device_id={"lon": peer}, device_id_type=MESH,
        )

    def gather_whole(kind, cross, count):
        rows = pl.ds(256 * kind, count * 32)
        return gather_copy(kind, rows, sibling, cross)

    for kind in range(4):

        @pl.when(own_class == kind)
        def _():
            def one(step, carry):
                gather_copy(kind, peer_rows(ml), lax.rem(ml + 2 * step + 2, LN), 0).start()
                return carry

            lax.fori_loop(0, LN // 2 - 1, one, 0)

    def gather_forward():
        for kind in range(4):

            @pl.when(own_class == kind)
            def _():
                gather_whole(kind, 0, 3).wait_recv()

            @pl.when(own_class != kind)
            def _():
                gather_whole(kind, 0, 4).wait_recv()

            for chip in range(4):
                gather_copy(kind, peer_rows(kind * 8 + chip * 2 + lax.rem(ml, 2)), sibling, 1).start()

    def gather_finish():
        for kind in range(4):
            gather_whole(kind, 1, 4).wait_recv()

    def gather_drain():
        for kind in range(4):
            gather_whole(kind, 1, 4).wait_send()

            @pl.when(own_class == kind)
            def _():
                gather_whole(kind, 0, 8).wait_send()
                gather_whole(kind, 0, 7).wait_send()

    def columns(index, width):
        return pl.ds(pl.multiple_of(index * width, width), width)

    def to_lon(hop, s, src, dst):
        def swap(step, carry):
            u, lb = step // 2, step % 2
            parts = [
                ysc[pl.ds(pl.multiple_of(k * 32 + lb * 16, 16), 16), columns(u, 128)] for k in range(8)
            ]
            parts = exchange(parts, (1, 2, 4))
            for og in range(8):
                ssc[pl.ds(pl.multiple_of((u * 8 + og) * 32 + lb * 16, 16), 16), :] = parts[og]
            return carry

        repeat(8, swap)

        def pick(step, carry):
            peer = l_peer(step)
            src[s, peer_rows(peer), :] = ssc[pl.ds(peer, 32, stride=32), :]
            send_l(hop, s, src, dst, peer)
            return carry

        repeat(LN - 1, pick)
        dst[s, peer_rows(ml), :] = ssc[pl.ds(ml, 32, stride=32), :]

    def lat_first(s):
        whole_z(0, s, send0, recv0).wait_recv()
        if s == 0:
            start_z(0, 1, send0, recv0)
        for u in range(4):
            ysc[:, u * 128 : (u + 1) * 128] = dot(latp[...], recv0[s, :, u].reshape(256, 128), NN)
        to_lon(1, s, send1, recv1)

    def lon_columns(s, src):
        def turn(c, carry):
            block = src[s, columns(c, 128), :].T
            high, low = split(block)
            halves[0:128, columns(c, 128)] = high
            halves[128:256, columns(c, 128)] = low
            return carry

        repeat(8, turn)

    def lon_first(s):
        whole_l(1, s, send1, recv1).wait_recv()
        lon_columns(s, recv1)

        def prior_block(n, total):
            both = dot(halves[...], lonfull[columns(n, 256), :], NT)
            drawn = both[0:128] + both[128:256]
            left = mask[:, columns(n, 256)].astype(F32) * (obs[:, columns(n, 256)] - drawn)
            prior[s, :, columns(n, 256)] = drawn
            resid[s, :, columns(n, 256)] = left
            squares = jnp.sum(left * left, axis=0, keepdims=True)
            return total + squares[:, 0:128] + squares[:, 128:256]

        redsend[s, 0:1, :] = lax.fori_loop(0, 4, prior_block, jnp.zeros((1, 128), F32))

        def halve(n, carry):
            high, low = split(resid[s, :, columns(n, 256)])
            halves[0:128, columns(n, 256)] = high
            halves[128:256, columns(n, 256)] = low
            return carry

        repeat(4, halve)

        for step in range(4):
            n = lax.rem(ml // 8 + step, 4)
            both = dot(halves[...], lonfull[:, columns(n, 256)], NN)
            summed = both[0:128] + both[128:256]
            for part in range(2):
                rows = pl.ds(pl.multiple_of(n * 256 + part * 128, 128), 128)
                send2[s, rows, :] = summed[:, part * 128 : (part + 1) * 128].T.astype(BF16)

            def one(k, carry):
                send_l(2, s, send2, recv2, n * 8 + lax.rem(ml + k, 8))
                return carry

            lax.fori_loop(1 if step == 0 else 0, 8, one, 0)
        recv2[s, peer_rows(ml), :] = send2[s, peer_rows(ml), :]

    def lat_back(s):
        whole_l(2, s, send2, recv2).wait_recv()
        ssc[...] = recv2[s].astype(F32)

        def swap(step, carry):
            u, lb = step // 2, step % 2
            parts = [ssc[pl.ds(lb * 512 + u * 8 + pg, 16, stride=32), :] for pg in range(8)]
            parts = exchange(parts, (1, 2, 4))
            for k in range(8):
                rows = pl.ds(pl.multiple_of(k * 32 + lb * 16, 16), 16)
                xd[rows, columns(u, 128)] = parts[k].astype(BF16)
            return carry

        repeat(8, swap)
        for n in range(2):
            cols = slice(n * 256, (n + 1) * 256)
            ysc[:, cols] = dot(latqt[...], xd[:, cols], NN)

        def turn(step, carry):
            u, ib = step // 2, step % 2
            parts = [ysc[pl.ds(pl.multiple_of(bb * 16 + ib * 8, 8), 8), columns(u, 128)] for bb in range(16)]
            parts = exchange(parts, (8, 16, 32, 64))
            for h in range(16):
                ssc[pl.ds(pl.multiple_of((u * 16 + h) * 16 + ib * 8, 8), 8), :] = parts[h]
            return carry

        repeat(8, turn)

        def picked(peer, u):
            return ssc[pl.ds(u * 256 + peer, 16, stride=16), :].astype(BF16)

        def pick(step, carry):
            peer = z_peer(step)
            for u in range(4):
                send3[s, peer, u] = picked(peer, u)
            send_z(3, s, send3, recv3, peer)
            return carry

        repeat(ZN - 1, pick)
        for u in range(4):
            recv3[s, mz, u] = picked(mz, u)

    def hours_mix(s):
        whole_z(3, s, send3, recv3).wait_recv()
        total = jnp.zeros((1, 128), F32)
        for u in range(4):
            cells = recv3[s, :, u].reshape(256, 128)
            both = dot(hour[...], cells, NN)
            mixed = both[0:256] + both[256:512]
            total = total + jnp.sum(mixed * cells.astype(F32), axis=0, keepdims=True)
            send4[s, :, u] = mixed.astype(BF16).reshape(16, 16, 128)
        redsend[s, 1:2, :] = total

        def one(step, carry):
            peer = z_peer(step)
            pltpu.make_async_remote_copy(
                src_ref=redsend.at[s], dst_ref=redz.at[s, mz],
                send_sem=send_sem.at[6, s], recv_sem=recv_sem.at[6, s],
                device_id={"tm": peer}, device_id_type=MESH,
            ).start()
            return carry

        lax.fori_loop(0, ZN - 1, one, 0)
        redz[s, mz] = redsend[s]
        start_z(4, s, send4, recv4)

    def sums_lon(s):
        whole_z(6, s, redz, redz).wait_recv()
        redmid[s] = jnp.sum(redz[s], axis=0)

        def one(step, carry):
            pltpu.make_async_remote_copy(
                src_ref=redmid.at[s], dst_ref=redl.at[s, ml],
                send_sem=send_sem.at[7, s], recv_sem=recv_sem.at[7, s],
                device_id={"lon": l_peer(step)}, device_id_type=MESH,
            ).start()
            return carry

        lax.fori_loop(0, LN - 1, one, 0)
        redl[s, ml] = redmid[s]

    def sums_whole(s):
        part = redl.at[s, pl.ds(0, LN - 1)]
        return pltpu.make_async_remote_copy(
            src_ref=part, dst_ref=part, send_sem=send_sem.at[7, s], recv_sem=recv_sem.at[7, s],
            device_id={"lon": l_peer(0)}, device_id_type=MESH,
        )

    def lat_last(s):
        whole_z(4, s, send4, recv4).wait_recv()

        def widen(i, carry):
            ssc[pl.ds(pl.multiple_of(i * 64, 64), 64), :] = recv4[s, i].reshape(64, 128).astype(F32)
            return carry

        repeat(ZN, widen)

        def turn(u, carry):
            parts = [ssc[pl.ds(u * 16 + h, 16, stride=64), :] for h in range(16)]
            parts = exchange(parts, (8, 16, 32, 64))
            for bb in range(16):
                xd[pl.ds(bb * 16, 16), columns(u, 128)] = parts[bb].astype(BF16)
            return carry

        repeat(4, turn)
        for n in range(2):
            cols = slice(n * 256, (n + 1) * 256)
            ysc[:, cols] = dot(latq[...], xd[:, cols], NN)
        to_lon(5, s, send5, recv5)

    def lon_last(s):
        sums_whole(s).wait_recv()
        total = jnp.sum(redl[s], axis=0)
        norm_sq = jnp.sum(total[0:1], axis=1, keepdims=True)
        quad = jnp.sum(total[1:2], axis=1, keepdims=True)
        step_size = norm_sq / (quad + NOISE_VAR * norm_sq)
        whole_l(5, s, send5, recv5).wait_recv()
        lon_columns(s, recv5)

        def block(n, carry):
            both = dot(halves[...], lonfull[columns(n, 256), :], NT)
            applied = both[0:128] + both[128:256]
            left = resid[s, :, columns(n, 256)]
            operated = mask[:, columns(n, 256)].astype(F32) * applied + NOISE_VAR * left
            prior[s, :, columns(n, 256)] += step_size * applied
            resid[s, :, columns(n, 256)] = left - step_size * operated
            return carry

        repeat(4, block)

    def results(s):
        return [
            pltpu.make_async_copy(src.at[s], dst.at[s], local_sem.at[9 + 2 * s + index])
            for index, (src, dst) in enumerate([(prior, post), (resid, nxt)])
        ]

    lat_first(0)
    gather_forward()
    gather_finish()
    lon_first(0)
    lat_first(1)
    lat_back(0)
    lon_first(1)
    lat_back(1)
    hours_mix(0)
    hours_mix(1)
    lat_last(0)
    sums_lon(0)
    sums_lon(1)
    lat_last(1)
    lon_last(0)
    for copy in results(0):
        copy.start()
    lon_last(1)
    for copy in results(1):
        copy.start()

    gather_drain()
    for s in range(2):
        whole_z(0, s, send0, recv0).wait_send()
        whole_l(1, s, send1, recv1).wait_send()
        whole_l(2, s, send2, recv2).wait_send()
        whole_z(3, s, send3, recv3).wait_send()
        whole_z(4, s, send4, recv4).wait_send()
        whole_l(5, s, send5, recv5).wait_send()
        whole_z(6, s, redz, redz).wait_send()
        sums_whole(s).wait_send()
        for copy in results(s):
            copy.wait()


def trig(step, period, count, columns):
    angle = 2.0 * np.pi * ((step * np.arange(count)[:, None] * np.arange(columns)[None]) % period) / period
    return np.concatenate([np.cos(angle), np.sin(angle)]).astype(np.float32)


def shards(noise, observed, mask, lat_factor, lon_factor, spectrum):
    periods = noise.shape[3]
    powers = jnp.concatenate([spectrum, spectrum[1:-1][::-1]])
    amplitude = jnp.sqrt(powers / periods)[None]
    coarse = jnp.asarray(trig(16, 512, 16, 512))
    fine = jnp.asarray(trig(1, 512, 16, 512))
    vmem = pl.BlockSpec(memory_space=pltpu.VMEM)
    hbm = pl.BlockSpec(memory_space=pltpu.HBM)
    zbuf = pltpu.VMEM((2, 16, 4, 16, 128), BF16)
    lbuf = pltpu.VMEM((2, 1024, 128), F32)
    lhalf = pltpu.VMEM((2, 1024, 128), BF16)
    scratch = [
        pltpu.VMEM((2, 16, 32, 512), BF16),
        pltpu.VMEM((256, 256), BF16),
        pltpu.VMEM((32, 1024), BF16),
        pltpu.VMEM((32, 512), F32),
        pltpu.VMEM((32, 512), F32),
        pltpu.VMEM((128, 1024), F32),
        pltpu.VMEM((128, 1024), jnp.int32),
        pltpu.VMEM((2, 2, 128, 1024), BF16),
        pltpu.VMEM((2, 256, 1024), BF16),
        pltpu.VMEM((512, 128), F32),
        pltpu.VMEM((256, 512), F32),
        pltpu.VMEM((1024, 128), F32),
        pltpu.VMEM((512, 128), F32),
        pltpu.VMEM((256, 256), BF16),
        pltpu.VMEM((256, 256), BF16),
        pltpu.VMEM((256, 256), BF16),
        pltpu.VMEM((512, 256), BF16),
        pltpu.VMEM((1024, 1024), BF16),
        pltpu.VMEM((256, 1024), BF16),
        pltpu.VMEM((256, 512), BF16),
        pltpu.VMEM((2, 128, 1024), F32),
        pltpu.VMEM((2, 128, 1024), F32),
        zbuf, zbuf, lbuf, lbuf, lhalf, lhalf, zbuf, zbuf, zbuf, zbuf, lbuf, lbuf,
        pltpu.VMEM((2, 8, 128), F32),
        pltpu.VMEM((2, 16, 8, 128), F32),
        pltpu.VMEM((2, 8, 128), F32),
        pltpu.VMEM((2, 32, 8, 128), F32),
        pltpu.SemaphoreType.DMA((HOPS, 2)),
        pltpu.SemaphoreType.DMA((HOPS, 2)),
        pltpu.SemaphoreType.DMA((2, 4)),
        pltpu.SemaphoreType.DMA((2, 4)),
        pltpu.SemaphoreType.DMA((13,)),
    ]
    out = jax.ShapeDtypeStruct((2, 128, 1024), F32)
    post, nxt = pl.pallas_call(
        body,
        out_shape=(out, out),
        in_specs=[hbm] * 5 + [vmem] + [hbm] * 2,
        out_specs=(hbm, hbm),
        scratch_shapes=scratch,
        compiler_params=pltpu.CompilerParams(
            collective_id=0, has_side_effects=True, vmem_limit_bytes=58 << 20
        ),
        name="posterior",
    )(
        noise, observed.reshape(128, 1024), mask.reshape(128, 1024), lat_factor, lon_factor, amplitude, coarse, fine
    )
    return post.reshape(2, 16, 8, 1024), nxt.reshape(2, 16, 8, 1024)


def solution(mesh):
    return jax.shard_map(
        shards,
        mesh=mesh,
        in_specs=(
            P(None, "tm", "lon", None),
            P("tm", "lon", None),
            P("tm", "lon", None),
            P(),
            P("lon", None),
            P(),
        ),
        out_specs=(P(None, "tm", "lon", None), P(None, "tm", "lon", None)),
        check_vma=False,
    )
```

```python
import functools

import jax
import jax.numpy as jnp
import numpy as np
from jax import lax
from jax.experimental import pallas as pl
from jax.experimental.pallas import tpu as pltpu
from jax.sharding import PartitionSpec as P

F32 = jnp.float32
BF16 = jnp.bfloat16
MESH = pl.DeviceIdType.MESH
NOISE_VAR = 0.25
NT = (((1,), (1,)), ((), ()))
NN = (((1,), (0,)), ((), ()))
HOPS = 8
ZN = 16
LN = 32


def repeat(count, step):
    lax.fori_loop(0, count, step, 0, unroll=min(count, 8))


def dot(left, right, dims):
    return lax.dot_general(left, right, dims, preferred_element_type=F32)


def split(value):
    high = value.astype(BF16)
    return high, (value - high.astype(F32)).astype(BF16)


def exchange(parts, strides):
    parts = list(parts)
    lane = lax.broadcasted_iota(jnp.int32, parts[0].shape, 1)
    for bit, stride in enumerate(strides):
        low_lanes = (lane & stride) == 0
        for first in range(len(parts)):
            if first & (1 << bit):
                continue
            second = first | (1 << bit)
            low, high = parts[first], parts[second]
            parts[first] = jnp.where(low_lanes, low, pltpu.roll(high, stride, 1))
            parts[second] = jnp.where(low_lanes, pltpu.roll(low, 128 - stride, 1), high)
    return parts


def body(
    noise_hbm, obs_hbm, mask_hbm, lat_hbm, lon_hbm, spec_hbm, coarse_hbm, fine_hbm,
    post, nxt,
    noise, lat, lon, coarse, fine, spec, obs, mask, tab, waves, work, ysc, ssc, tsc, lat32, latp, latq, latqt, hour,
    lonfull, halves, xd, prior, resid,
    send0, recv0, send1, recv1, send2, recv2, send3, recv3, send4, recv4, send5, recv5,
    redsend, redz, redmid, redl,
    send_sem, recv_sem, gather_send, gather_recv, local_sem,
):
    mz = lax.axis_index("tm")
    ml = lax.axis_index("lon")

    def z_peer(step):
        away = (8 - (step + 1) // 2) * (1 - 2 * (step % 2))
        return lax.rem(mz + away + ZN, ZN)

    def l_peer(step):
        return lax.rem(ml + step + 1, LN)

    fetches = [
        pltpu.make_async_copy(src, dst, local_sem.at[index])
        for index, (src, dst) in enumerate(
            [(coarse_hbm, coarse), (fine_hbm, fine), (noise_hbm, noise), (lat_hbm, lat), (lon_hbm, lon), (spec_hbm, spec),
             (obs_hbm, obs), (mask_hbm, mask)]
        )
    ]
    for fetch in fetches:
        fetch.start()
    barrier = pltpu.get_barrier_semaphore()

    def greet_z(step, carry):
        pl.semaphore_signal(barrier, inc=1, device_id={"tm": z_peer(step)}, device_id_type=MESH)
        return carry

    def greet_l(step, carry):
        pl.semaphore_signal(barrier, inc=1, device_id={"lon": l_peer(step)}, device_id_type=MESH)
        return carry

    lax.fori_loop(0, ZN - 1, greet_z, 0)
    lax.fori_loop(0, LN - 1, greet_l, 0)

    def send_z(hop, s, half, src, dst, peer):
        pltpu.make_async_remote_copy(
            src_ref=src.at[s, half, peer], dst_ref=dst.at[s, half, mz],
            send_sem=send_sem.at[hop, s, half], recv_sem=recv_sem.at[hop, s, half],
            device_id={"tm": peer}, device_id_type=MESH,
        ).start()

    def start_z(hop, s, half, src, dst):
        def one(step, carry):
            send_z(hop, s, half, src, dst, z_peer(step))
            return carry

        lax.fori_loop(0, ZN - 1, one, 0)
        dst[s, half, mz] = src[s, half, mz]

    def whole_z(hop, s, half, src, dst):
        return pltpu.make_async_remote_copy(
            src_ref=src.at[s, half, pl.ds(0, ZN - 1)], dst_ref=dst.at[s, half, pl.ds(0, ZN - 1)],
            send_sem=send_sem.at[hop, s, half], recv_sem=recv_sem.at[hop, s, half],
            device_id={"tm": z_peer(0)}, device_id_type=MESH,
        )

    def peer_rows(peer, count=32):
        return pl.ds(pl.multiple_of(peer * count, count), count)

    def send_l(hop, s, half, src, dst, peer):
        count = src.shape[2] // LN
        pltpu.make_async_remote_copy(
            src_ref=src.at[s, half, peer_rows(peer, count)], dst_ref=dst.at[s, half, peer_rows(ml, count)],
            send_sem=send_sem.at[hop, s, half], recv_sem=recv_sem.at[hop, s, half],
            device_id={"lon": peer}, device_id_type=MESH,
        ).start()

    def whole_l(hop, s, half, src, dst):
        rows = pl.ds(0, src.shape[2] // LN * (LN - 1))
        return pltpu.make_async_remote_copy(
            src_ref=src.at[s, half, rows], dst_ref=dst.at[s, half, rows],
            send_sem=send_sem.at[hop, s, half], recv_sem=recv_sem.at[hop, s, half],
            device_id={"lon": l_peer(0)}, device_id_type=MESH,
        )

    for fetch in fetches[:6]:
        fetch.wait()
    order = lax.broadcasted_iota(jnp.int32, (257, 512), 1)
    picks = (jnp.minimum(order, 512 - order) == lax.broadcasted_iota(jnp.int32, (257, 512), 0)).astype(F32)
    powers = lax.dot_general(
        spec[...].reshape(1, 257), picks, NN, precision=lax.Precision.HIGHEST, preferred_element_type=F32
    )
    amp_row = jnp.sqrt(powers / 512)

    def tables(group):
        base = pl.multiple_of(group * 8, 8)
        c1 = coarse[pl.ds(base, 8), :]
        s1 = coarse[pl.ds(16 + base, 8), :]
        for pair in range(8):
            cos_rows, sin_rows = [], []
            for hh in (2 * pair, 2 * pair + 1):
                c2, s2 = fine[hh : hh + 1, :], fine[16 + hh : 17 + hh, :]
                cos_rows.append((c1 * c2 - s1 * s2) * amp_row)
                sin_rows.append((s1 * c2 + c1 * s2) * amp_row)
            cw = jnp.concatenate(cos_rows, axis=0).astype(BF16)
            sw = jnp.concatenate(sin_rows, axis=0).astype(BF16)
            rows = pl.ds(pair * 16, 16)
            tab[0, group, rows, 0:512] = cw
            tab[0, group, rows, 512:1024] = sw
            tab[1, group, rows, 0:512] = -sw
            tab[1, group, rows, 512:1024] = cw

    def tables_loop(group, carry):
        tables(group)
        return carry

    lax.fori_loop(0, 2, tables_loop, 0)

    def transform(s):
        def one(group, carry):
            for part in range(2):
                rows = noise[part].reshape(512, 512)
                term = dot(rows, tab[s, group, :, part * 512 : (part + 1) * 512], NT)
                if part == 0:
                    work[0:512, :] = term
                else:
                    work[0:512, :] += term

            def swap(u, inner):
                parts = [work[pl.ds(u * 8 + og, 16, stride=32), :] for og in range(8)]
                parts = exchange(parts, (1, 2, 4))
                for jl in range(8):
                    send0[s, u // 2, group * 8 + jl, u % 2] = parts[jl].astype(BF16)
                return inner

            repeat(4, swap)
            return carry

        lax.fori_loop(0, 2, one, 0)

    transform(0)
    transform(1)

    def spread(value):
        lat32[0:256, :] = value[:, 0:128]
        lat32[256:512, :] = value[:, 128:256]

    spread(lat[...].astype(F32))
    for k in range(8):
        latp[k * 32 : (k + 1) * 32, :] = jnp.concatenate(
            [lat32[pl.ds(c * 256 + k, 32, stride=8), :] for c in range(2)], axis=1
        ).astype(BF16)
    spread(latp[...].astype(F32).T)
    for bb in range(16):
        latqt[bb * 16 : (bb + 1) * 16, :] = jnp.concatenate(
            [lat32[pl.ds(c * 256 + bb, 16, stride=16), :] for c in range(2)], axis=1
        ).astype(BF16)
    latq[...] = latqt[...].astype(F32).T.astype(BF16)

    def wave(j, carry):
        c1 = coarse[pl.ds(j, 1), :] * amp_row
        s1 = coarse[pl.ds(16 + j, 1), :] * amp_row
        c2, s2 = fine[0:16, :], fine[16:32, :]
        rows = pl.ds(pl.multiple_of(j * 16, 16), 16)
        for part, value in enumerate((c1 * c2 - s1 * s2, s1 * c2 + c1 * s2)):
            high, low = split(value)
            waves[0, rows, part * 512 : (part + 1) * 512] = high
            waves[1, rows, part * 512 : (part + 1) * 512] = low
        return carry

    lax.fori_loop(0, ZN, wave, 0)
    cross = dot(waves[0], waves[1], NT)
    kernel = dot(waves[0], waves[0], NT) + (cross + cross.T)
    high, low = split(kernel)
    hour[0:256, :] = high
    hour[256:512, :] = low
    redsend[...] = jnp.zeros_like(redsend)
    fetches[6].wait()
    fetches[7].wait()

    lonfull[peer_rows(ml), :] = lon[...]
    for kind in range(3):
        rest = 1024 - 256 * (kind + 1)
        lonfull[256 * kind : 256 * (kind + 1), 1024 - rest :] = jnp.zeros((256, rest), BF16)
    pl.semaphore_wait(barrier, ZN + LN - 2)
    start_z(0, 0, 0, send0, recv0)
    start_z(0, 0, 1, send0, recv0)

    sibling = ml + 1 - 2 * lax.rem(ml, 2)
    own_class = ml // 8

    def gather_copy(kind, rows, peer, cross):
        width = 256 * (kind + 1)
        return pltpu.make_async_remote_copy(
            src_ref=lonfull.at[rows, pl.ds(0, width)], dst_ref=lonfull.at[rows, pl.ds(0, width)],
            send_sem=gather_send.at[cross, kind], recv_sem=gather_recv.at[cross, kind],
            device_id={"lon": peer}, device_id_type=MESH,
        )

    def gather_whole(kind, cross, count):
        rows = pl.ds(256 * kind, count * 32)
        return gather_copy(kind, rows, sibling, cross)

    for kind in range(4):

        @pl.when(own_class == kind)
        def _():
            def one(step, carry):
                gather_copy(kind, peer_rows(ml), lax.rem(ml + 2 * step + 2, LN), 0).start()
                return carry

            lax.fori_loop(0, LN // 2 - 1, one, 0)

    def gather_forward():
        for kind in range(4):

            @pl.when(own_class == kind)
            def _():
                gather_whole(kind, 0, 3).wait_recv()

            @pl.when(own_class != kind)
            def _():
                gather_whole(kind, 0, 4).wait_recv()

            for chip in range(4):
                gather_copy(kind, peer_rows(kind * 8 + chip * 2 + lax.rem(ml, 2)), sibling, 1).start()

    def gather_finish():
        for kind in range(4):
            gather_whole(kind, 1, 4).wait_recv()

    def gather_drain():
        for kind in range(4):
            gather_whole(kind, 1, 4).wait_send()

            @pl.when(own_class == kind)
            def _():
                gather_whole(kind, 0, 8).wait_send()
                gather_whole(kind, 0, 7).wait_send()

    def columns(index, width):
        return pl.ds(pl.multiple_of(index * width, width), width)

    def to_lon(hop, s, half, src, dst):
        def swap(step, carry):
            v, lb = step // 2, step % 2
            parts = [
                ysc[pl.ds(pl.multiple_of(k * 32 + lb * 16, 16), 16), columns(v, 128)] for k in range(8)
            ]
            parts = exchange(parts, (1, 2, 4))
            for og in range(8):
                ssc[pl.ds(pl.multiple_of((v * 8 + og) * 32 + lb * 16, 16), 16), :] = parts[og]
            return carry

        repeat(4, swap)

        def pick(step, carry):
            peer = l_peer(step)
            src[s, half, peer_rows(peer, 16), :] = ssc[pl.ds(peer, 16, stride=32), :]
            send_l(hop, s, half, src, dst, peer)
            return carry

        repeat(LN - 1, pick)
        dst[s, half, peer_rows(ml, 16), :] = ssc[pl.ds(ml, 16, stride=32), :]

    def lat_first(s, half):
        whole_z(0, s, half, send0, recv0).wait_recv()
        if s == 0:
            start_z(0, 1, half, send0, recv0)
        cells = jnp.concatenate([recv0[s, half, :, v].reshape(256, 128) for v in range(2)], axis=1)
        ysc[...] = dot(latp[...], cells, NN)
        to_lon(1, s, half, send1, recv1)

    def lon_columns(s, src):
        def turn(c, carry):
            block = jnp.concatenate(
                [src[s, half, peer_rows(c * 4 + i, 16), :] for i in range(4) for half in range(2)], axis=0
            ).T
            high, low = split(block)
            halves[0:128, columns(c, 128)] = high
            halves[128:256, columns(c, 128)] = low
            return carry

        repeat(8, turn)

    def lon_first(s):
        for half in range(2):
            whole_l(1, s, half, send1, recv1).wait_recv()
        lon_columns(s, recv1)

        def prior_block(n, total):
            both = dot(halves[...], lonfull[columns(n, 256), :], NT)
            drawn = both[0:128] + both[128:256]
            left = mask[:, columns(n, 256)].astype(F32) * (obs[:, columns(n, 256)] - drawn)
            prior[s, :, columns(n, 256)] = drawn
            resid[s, :, columns(n, 256)] = left
            squares = jnp.sum(left * left, axis=0, keepdims=True)
            return total + squares[:, 0:128] + squares[:, 128:256]

        redsend[s, 0:1, :] = lax.fori_loop(0, 4, prior_block, jnp.zeros((1, 128), F32))

        def halve(n, carry):
            high, low = split(resid[s, :, columns(n, 256)])
            halves[0:128, columns(n, 256)] = high
            halves[128:256, columns(n, 256)] = low
            return carry

        repeat(4, halve)

        for step in range(4):
            n = lax.rem(ml // 8 + step, 4)
            both = dot(halves[...], lonfull[:, columns(n, 256)], NN)
            summed = both[0:128] + both[128:256]
            for part in range(2):
                rows = pl.ds(pl.multiple_of(n * 256 + part * 128, 128), 128)
                send2[s, 0, rows, :] = summed[:, part * 128 : (part + 1) * 128].T.astype(BF16)

            def one(k, carry):
                send_l(2, s, 0, send2, recv2, n * 8 + lax.rem(ml + k, 8))
                return carry

            lax.fori_loop(1 if step == 0 else 0, 8, one, 0)
        recv2[s, 0, peer_rows(ml), :] = send2[s, 0, peer_rows(ml), :]

    def lat_back(s):
        whole_l(2, s, 0, send2, recv2).wait_recv()
        ssc[...] = recv2[s, 0].astype(F32)
        for half in range(2):

            def swap(step, carry):
                v, lb = step // 2, step % 2
                base = lb * 512 + half * 16 + v * 8
                parts = [ssc[pl.ds(base + pg, 16, stride=32), :] for pg in range(8)]
                parts = exchange(parts, (1, 2, 4))
                for k in range(8):
                    rows = pl.ds(pl.multiple_of(k * 32 + lb * 16, 16), 16)
                    xd[rows, columns(v, 128)] = parts[k].astype(BF16)
                return carry

            repeat(4, swap)
            ysc[...] = dot(latqt[...], xd[...], NN)

            def turn(step, carry):
                v, ib = step // 2, step % 2
                parts = [
                    ysc[pl.ds(pl.multiple_of(bb * 16 + ib * 8, 8), 8), columns(v, 128)] for bb in range(16)
                ]
                parts = exchange(parts, (8, 16, 32, 64))
                for h in range(16):
                    tsc[pl.ds(pl.multiple_of((v * 16 + h) * 16 + ib * 8, 8), 8), :] = parts[h]
                return carry

            repeat(4, turn)

            def picked(peer, v):
                return tsc[pl.ds(v * 256 + peer, 16, stride=16), :].astype(BF16)

            def pick(step, carry):
                peer = z_peer(step)
                for v in range(2):
                    send3[s, half, peer, v] = picked(peer, v)
                send_z(3, s, half, send3, recv3, peer)
                return carry

            repeat(ZN - 1, pick)
            for v in range(2):
                recv3[s, half, mz, v] = picked(mz, v)

    quads = {}

    def hours_mix(s, half):
        whole_z(3, s, half, send3, recv3).wait_recv()
        cells = jnp.concatenate([recv3[s, half, :, v].reshape(256, 128) for v in range(2)], axis=1)
        both = dot(hour[...], cells, NN)
        mixed = both[0:256] + both[256:512]
        total = jnp.sum(mixed * cells.astype(F32), axis=0, keepdims=True)
        quads[s, half] = total[:, 0:128] + total[:, 128:256]
        for v in range(2):
            send4[s, half, :, v] = mixed[:, v * 128 : (v + 1) * 128].astype(BF16).reshape(16, 16, 128)
        if half == 1:
            redsend[s, 1:2, :] = quads[s, 0] + quads[s, 1]

            def one(step, carry):
                pltpu.make_async_remote_copy(
                    src_ref=redsend.at[s], dst_ref=redz.at[s, mz],
                    send_sem=send_sem.at[6, s, 0], recv_sem=recv_sem.at[6, s, 0],
                    device_id={"tm": z_peer(step)}, device_id_type=MESH,
                ).start()
                return carry

            lax.fori_loop(0, ZN - 1, one, 0)
            redz[s, mz] = redsend[s]
        start_z(4, s, half, send4, recv4)

    def sums_z_whole(s):
        part = redz.at[s, pl.ds(0, ZN - 1)]
        return pltpu.make_async_remote_copy(
            src_ref=part, dst_ref=part, send_sem=send_sem.at[6, s, 0], recv_sem=recv_sem.at[6, s, 0],
            device_id={"tm": z_peer(0)}, device_id_type=MESH,
        )

    def sums_lon(s):
        sums_z_whole(s).wait_recv()
        redmid[s] = jnp.sum(redz[s], axis=0)

        def one(step, carry):
            pltpu.make_async_remote_copy(
                src_ref=redmid.at[s], dst_ref=redl.at[s, ml],
                send_sem=send_sem.at[7, s, 0], recv_sem=recv_sem.at[7, s, 0],
                device_id={"lon": l_peer(step)}, device_id_type=MESH,
            ).start()
            return carry

        lax.fori_loop(0, LN - 1, one, 0)
        redl[s, ml] = redmid[s]

    def sums_whole(s):
        part = redl.at[s, pl.ds(0, LN - 1)]
        return pltpu.make_async_remote_copy(
            src_ref=part, dst_ref=part, send_sem=send_sem.at[7, s, 0], recv_sem=recv_sem.at[7, s, 0],
            device_id={"lon": l_peer(0)}, device_id_type=MESH,
        )

    def lat_last(s, half):
        whole_z(4, s, half, send4, recv4).wait_recv()

        def widen(i, carry):
            ssc[peer_rows(i), :] = recv4[s, half, i].reshape(32, 128).astype(F32)
            return carry

        repeat(ZN, widen)

        def turn(v, carry):
            parts = [ssc[pl.ds(v * 16 + h, 16, stride=32), :] for h in range(16)]
            parts = exchange(parts, (8, 16, 32, 64))
            for bb in range(16):
                xd[pl.ds(bb * 16, 16), columns(v, 128)] = parts[bb].astype(BF16)
            return carry

        repeat(2, turn)
        ysc[...] = dot(latq[...], xd[...], NN)
        to_lon(5, s, half, send5, recv5)

    def lon_last(s):
        sums_whole(s).wait_recv()
        total = jnp.sum(redl[s], axis=0)
        norm_sq = jnp.sum(total[0:1], axis=1, keepdims=True)
        quad = jnp.sum(total[1:2], axis=1, keepdims=True)
        step_size = norm_sq / (quad + NOISE_VAR * norm_sq)
        for half in range(2):
            whole_l(5, s, half, send5, recv5).wait_recv()
        lon_columns(s, recv5)

        def block(n, carry):
            both = dot(halves[...], lonfull[columns(n, 256), :], NT)
            applied = both[0:128] + both[128:256]
            left = resid[s, :, columns(n, 256)]
            operated = mask[:, columns(n, 256)].astype(F32) * applied + NOISE_VAR * left
            prior[s, :, columns(n, 256)] += step_size * applied
            resid[s, :, columns(n, 256)] = left - step_size * operated
            return carry

        repeat(4, block)

    def results(s):
        return [
            pltpu.make_async_copy(src.at[s], dst.at[s], local_sem.at[10 + 2 * s + index])
            for index, (src, dst) in enumerate([(prior, post), (resid, nxt)])
        ]

    lat_first(0, 0)
    lat_first(0, 1)
    gather_forward()
    gather_finish()
    lon_first(0)
    lat_first(1, 0)
    lat_first(1, 1)
    lat_back(0)
    lon_first(1)
    hours_mix(0, 0)
    lat_back(1)
    hours_mix(0, 1)
    hours_mix(1, 0)
    hours_mix(1, 1)
    lat_last(0, 0)
    lat_last(0, 1)
    sums_lon(0)
    sums_lon(1)
    lat_last(1, 0)
    lon_last(0)
    for copy in results(0):
        copy.start()
    lat_last(1, 1)
    lon_last(1)
    for copy in results(1):
        copy.start()

    gather_drain()
    for s in range(2):
        for half in range(2):
            whole_z(0, s, half, send0, recv0).wait_send()
            whole_l(1, s, half, send1, recv1).wait_send()
            whole_z(3, s, half, send3, recv3).wait_send()
            whole_z(4, s, half, send4, recv4).wait_send()
            whole_l(5, s, half, send5, recv5).wait_send()
        whole_l(2, s, 0, send2, recv2).wait_send()
        sums_z_whole(s).wait_send()
        sums_whole(s).wait_send()
        for copy in results(s):
            copy.wait()


def trig(step, period, count, columns):
    angle = 2.0 * np.pi * ((step * np.arange(count)[:, None] * np.arange(columns)[None]) % period) / period
    return np.concatenate([np.cos(angle), np.sin(angle)]).astype(np.float32)


def shards(noise, observed, mask, lat_factor, lon_factor, spectrum):
    periods = noise.shape[3]
    coarse = jnp.asarray(trig(16, 512, 16, 512))
    fine = jnp.asarray(trig(1, 512, 16, 512))
    vmem = pl.BlockSpec(memory_space=pltpu.VMEM)
    hbm = pl.BlockSpec(memory_space=pltpu.HBM)
    zbuf = pltpu.VMEM((2, 2, 16, 2, 16, 128), BF16)
    lbuf = pltpu.VMEM((2, 2, 512, 128), F32)
    lhalf = pltpu.VMEM((2, 1, 1024, 128), BF16)
    scratch = [
        pltpu.VMEM((2, 16, 32, 512), BF16),
        pltpu.VMEM((256, 256), BF16),
        pltpu.VMEM((32, 1024), BF16),
        pltpu.VMEM((32, 512), F32),
        pltpu.VMEM((32, 512), F32),
        pltpu.VMEM((257,), F32),
        pltpu.VMEM((128, 1024), F32),
        pltpu.VMEM((128, 1024), jnp.int32),
        pltpu.VMEM((2, 2, 128, 1024), BF16),
        pltpu.VMEM((2, 256, 1024), BF16),
        pltpu.VMEM((512, 128), F32),
        pltpu.VMEM((256, 256), F32),
        pltpu.VMEM((1024, 128), F32),
        pltpu.VMEM((512, 128), F32),
        pltpu.VMEM((512, 128), F32),
        pltpu.VMEM((256, 256), BF16),
        pltpu.VMEM((256, 256), BF16),
        pltpu.VMEM((256, 256), BF16),
        pltpu.VMEM((512, 256), BF16),
        pltpu.VMEM((1024, 1024), BF16),
        pltpu.VMEM((256, 1024), BF16),
        pltpu.VMEM((256, 256), BF16),
        pltpu.VMEM((2, 128, 1024), F32),
        pltpu.VMEM((2, 128, 1024), F32),
        zbuf, zbuf, lbuf, lbuf, lhalf, lhalf, zbuf, zbuf, zbuf, zbuf, lbuf, lbuf,
        pltpu.VMEM((2, 8, 128), F32),
        pltpu.VMEM((2, 16, 8, 128), F32),
        pltpu.VMEM((2, 8, 128), F32),
        pltpu.VMEM((2, 32, 8, 128), F32),
        pltpu.SemaphoreType.DMA((HOPS, 2, 2)),
        pltpu.SemaphoreType.DMA((HOPS, 2, 2)),
        pltpu.SemaphoreType.DMA((2, 4)),
        pltpu.SemaphoreType.DMA((2, 4)),
        pltpu.SemaphoreType.DMA((14,)),
    ]
    out = jax.ShapeDtypeStruct((2, 128, 1024), F32)
    post, nxt = pl.pallas_call(
        body,
        out_shape=(out, out),
        in_specs=[hbm] * 8,
        out_specs=(hbm, hbm),
        scratch_shapes=scratch,
        compiler_params=pltpu.CompilerParams(
            collective_id=0, has_side_effects=True, vmem_limit_bytes=58 << 20
        ),
        name="posterior",
    )(
        noise, observed.reshape(128, 1024), mask.reshape(128, 1024), lat_factor, lon_factor, spectrum, coarse, fine
    )
    return post.reshape(2, 16, 8, 1024), nxt.reshape(2, 16, 8, 1024)


def solution(mesh):
    return jax.shard_map(
        shards,
        mesh=mesh,
        in_specs=(
            P(None, "tm", "lon", None),
            P("tm", "lon", None),
            P("tm", "lon", None),
            P(),
            P("lon", None),
            P(),
        ),
        out_specs=(P(None, "tm", "lon", None), P(None, "tm", "lon", None)),
        check_vma=False,
    )
```

```python
import functools

import jax
import jax.numpy as jnp
import numpy as np
from jax import lax
from jax.experimental import pallas as pl
from jax.experimental.pallas import tpu as pltpu
from jax.sharding import PartitionSpec as P

F32 = jnp.float32
BF16 = jnp.bfloat16
MESH = pl.DeviceIdType.MESH
NOISE_VAR = 0.25
NT = (((1,), (1,)), ((), ()))
NN = (((1,), (0,)), ((), ()))
HOPS = 8
ZN = 16
LN = 32


def repeat(count, step):
    lax.fori_loop(0, count, step, 0, unroll=min(count, 8))


def dot(left, right, dims):
    return lax.dot_general(left, right, dims, preferred_element_type=F32)


def split(value):
    high = value.astype(BF16)
    return high, (value - high.astype(F32)).astype(BF16)


def exchange(parts, strides):
    parts = list(parts)
    lane = lax.broadcasted_iota(jnp.int32, parts[0].shape, 1)
    for bit, stride in enumerate(strides):
        low_lanes = (lane & stride) == 0
        for first in range(len(parts)):
            if first & (1 << bit):
                continue
            second = first | (1 << bit)
            low, high = parts[first], parts[second]
            parts[first] = jnp.where(low_lanes, low, pltpu.roll(high, stride, 1))
            parts[second] = jnp.where(low_lanes, pltpu.roll(low, 128 - stride, 1), high)
    return parts


def body(
    noise_hbm, obs_hbm, mask_hbm, lat_hbm, lon_hbm, spec_hbm, coarse_hbm, fine_hbm,
    post, nxt,
    noise, lat, lon, coarse, fine, spec, obs, mask, tab, waves, work, ysc, ssc, tsc, lat32, latp, latq, latqt, hour,
    lonfull, halves, xd, prior, resid,
    send0, recv0, send1, recv1, send2, recv2, send3, recv3, send4, recv4, send5, recv5,
    redsend, redz, redmid, redl,
    send_sem, recv_sem, gather_send, gather_recv, local_sem,
):
    mz = lax.axis_index("tm")
    ml = lax.axis_index("lon")

    def z_peer(step):
        away = (8 - (step + 1) // 2) * (1 - 2 * (step % 2))
        return lax.rem(mz + away + ZN, ZN)

    def l_peer(step):
        return lax.rem(ml + step + 1, LN)

    fetches = [
        pltpu.make_async_copy(src, dst, local_sem.at[index])
        for index, (src, dst) in enumerate(
            [(coarse_hbm, coarse), (fine_hbm, fine), (noise_hbm, noise), (lat_hbm, lat), (lon_hbm, lon), (spec_hbm, spec),
             (obs_hbm, obs), (mask_hbm, mask)]
        )
    ]
    for fetch in fetches:
        fetch.start()
    barrier = pltpu.get_barrier_semaphore()

    def greet_z(step, carry):
        pl.semaphore_signal(barrier, inc=1, device_id={"tm": z_peer(step)}, device_id_type=MESH)
        return carry

    def greet_l(step, carry):
        pl.semaphore_signal(barrier, inc=1, device_id={"lon": l_peer(step)}, device_id_type=MESH)
        return carry

    lax.fori_loop(0, ZN - 1, greet_z, 0)
    lax.fori_loop(0, LN - 1, greet_l, 0)

    def send_z(hop, s, half, src, dst, peer):
        pltpu.make_async_remote_copy(
            src_ref=src.at[s, half, peer], dst_ref=dst.at[s, half, mz],
            send_sem=send_sem.at[hop, s, half], recv_sem=recv_sem.at[hop, s, half],
            device_id={"tm": peer}, device_id_type=MESH,
        ).start()

    def start_z(hop, s, half, src, dst):
        def one(step, carry):
            send_z(hop, s, half, src, dst, z_peer(step))
            return carry

        lax.fori_loop(0, ZN - 1, one, 0, unroll=5)
        dst[s, half, mz] = src[s, half, mz]

    def whole_z(hop, s, half, src, dst):
        return pltpu.make_async_remote_copy(
            src_ref=src.at[s, half, pl.ds(0, ZN - 1)], dst_ref=dst.at[s, half, pl.ds(0, ZN - 1)],
            send_sem=send_sem.at[hop, s, half], recv_sem=recv_sem.at[hop, s, half],
            device_id={"tm": z_peer(0)}, device_id_type=MESH,
        )

    def peer_rows(peer, count=32):
        return pl.ds(pl.multiple_of(peer * count, count), count)

    def send_l(hop, s, half, src, dst, peer):
        count = src.shape[2] // LN
        pltpu.make_async_remote_copy(
            src_ref=src.at[s, half, peer_rows(peer, count)], dst_ref=dst.at[s, half, peer_rows(ml, count)],
            send_sem=send_sem.at[hop, s, half], recv_sem=recv_sem.at[hop, s, half],
            device_id={"lon": peer}, device_id_type=MESH,
        ).start()

    def whole_l(hop, s, half, src, dst):
        rows = pl.ds(0, src.shape[2] // LN * (LN - 1))
        return pltpu.make_async_remote_copy(
            src_ref=src.at[s, half, rows], dst_ref=dst.at[s, half, rows],
            send_sem=send_sem.at[hop, s, half], recv_sem=recv_sem.at[hop, s, half],
            device_id={"lon": l_peer(0)}, device_id_type=MESH,
        )

    for fetch in fetches[:6]:
        fetch.wait()
    order = lax.broadcasted_iota(jnp.int32, (257, 512), 1)
    picks = (jnp.minimum(order, 512 - order) == lax.broadcasted_iota(jnp.int32, (257, 512), 0)).astype(F32)
    powers = lax.dot_general(
        spec[...].reshape(1, 257), picks, NN, precision=lax.Precision.HIGHEST, preferred_element_type=F32
    )
    amp_row = jnp.sqrt(powers / 512)

    def tables(group):
        base = pl.multiple_of(group * 8, 8)
        c1 = coarse[pl.ds(base, 8), :]
        s1 = coarse[pl.ds(16 + base, 8), :]
        for pair in range(8):
            cos_rows, sin_rows = [], []
            for hh in (2 * pair, 2 * pair + 1):
                c2, s2 = fine[hh : hh + 1, :], fine[16 + hh : 17 + hh, :]
                cos_rows.append((c1 * c2 - s1 * s2) * amp_row)
                sin_rows.append((s1 * c2 + c1 * s2) * amp_row)
            cw = jnp.concatenate(cos_rows, axis=0).astype(BF16)
            sw = jnp.concatenate(sin_rows, axis=0).astype(BF16)
            rows = pl.ds(pair * 16, 16)
            tab[0, group, rows, 0:512] = cw
            tab[0, group, rows, 512:1024] = sw
            tab[1, group, rows, 0:512] = -sw
            tab[1, group, rows, 512:1024] = cw

    def tables_loop(group, carry):
        tables(group)
        return carry

    lax.fori_loop(0, 2, tables_loop, 0)

    def transform(s):
        def one(group, carry):
            for part in range(2):
                rows = noise[part].reshape(512, 512)
                term = dot(rows, tab[s, group, :, part * 512 : (part + 1) * 512], NT)
                if part == 0:
                    work[0:512, :] = term
                else:
                    work[0:512, :] += term

            def swap(u, inner):
                parts = [work[pl.ds(u * 8 + og, 16, stride=32), :] for og in range(8)]
                parts = exchange(parts, (1, 2, 4))
                for jl in range(8):
                    send0[s, u // 2, group * 8 + jl, u % 2] = parts[jl].astype(BF16)
                return inner

            repeat(4, swap)
            return carry

        lax.fori_loop(0, 2, one, 0)

    transform(0)
    transform(1)

    def spread(value):
        lat32[0:256, :] = value[:, 0:128]
        lat32[256:512, :] = value[:, 128:256]

    spread(lat[...].astype(F32))
    for k in range(8):
        latp[k * 32 : (k + 1) * 32, :] = jnp.concatenate(
            [lat32[pl.ds(c * 256 + k, 32, stride=8), :] for c in range(2)], axis=1
        ).astype(BF16)
    spread(latp[...].astype(F32).T)
    for bb in range(16):
        latqt[bb * 16 : (bb + 1) * 16, :] = jnp.concatenate(
            [lat32[pl.ds(c * 256 + bb, 16, stride=16), :] for c in range(2)], axis=1
        ).astype(BF16)
    latq[...] = latqt[...].astype(F32).T.astype(BF16)

    def wave(j, carry):
        c1 = coarse[pl.ds(j, 1), :] * amp_row
        s1 = coarse[pl.ds(16 + j, 1), :] * amp_row
        c2, s2 = fine[0:16, :], fine[16:32, :]
        rows = pl.ds(pl.multiple_of(j * 16, 16), 16)
        for part, value in enumerate((c1 * c2 - s1 * s2, s1 * c2 + c1 * s2)):
            high, low = split(value)
            waves[0, rows, part * 512 : (part + 1) * 512] = high
            waves[1, rows, part * 512 : (part + 1) * 512] = low
        return carry

    lax.fori_loop(0, ZN, wave, 0)
    cross = dot(waves[0], waves[1], NT)
    kernel = dot(waves[0], waves[0], NT) + (cross + cross.T)
    high, low = split(kernel)
    hour[0:256, :] = high
    hour[256:512, :] = low
    redsend[...] = jnp.zeros_like(redsend)
    fetches[6].wait()
    fetches[7].wait()

    lonfull[peer_rows(ml), :] = lon[...]
    for kind in range(3):
        rest = 1024 - 256 * (kind + 1)
        lonfull[256 * kind : 256 * (kind + 1), 1024 - rest :] = jnp.zeros((256, rest), BF16)
    pl.semaphore_wait(barrier, ZN + LN - 2)
    start_z(0, 0, 0, send0, recv0)
    start_z(0, 0, 1, send0, recv0)

    sibling = ml + 1 - 2 * lax.rem(ml, 2)
    own_class = ml // 8

    def gather_copy(kind, rows, peer, cross):
        width = 256 * (kind + 1)
        return pltpu.make_async_remote_copy(
            src_ref=lonfull.at[rows, pl.ds(0, width)], dst_ref=lonfull.at[rows, pl.ds(0, width)],
            send_sem=gather_send.at[cross, kind], recv_sem=gather_recv.at[cross, kind],
            device_id={"lon": peer}, device_id_type=MESH,
        )

    def gather_whole(kind, cross, count):
        rows = pl.ds(256 * kind, count * 32)
        return gather_copy(kind, rows, sibling, cross)

    for kind in range(4):

        @pl.when(own_class == kind)
        def _():
            def one(step, carry):
                gather_copy(kind, peer_rows(ml), lax.rem(ml + 2 * step + 2, LN), 0).start()
                return carry

            lax.fori_loop(0, LN // 2 - 1, one, 0)

    def gather_forward():
        for kind in range(4):

            @pl.when(own_class == kind)
            def _():
                gather_whole(kind, 0, 3).wait_recv()

            @pl.when(own_class != kind)
            def _():
                gather_whole(kind, 0, 4).wait_recv()

            for chip in range(4):
                gather_copy(kind, peer_rows(kind * 8 + chip * 2 + lax.rem(ml, 2)), sibling, 1).start()

    def gather_finish():
        for kind in range(4):
            gather_whole(kind, 1, 4).wait_recv()

    def gather_drain():
        for kind in range(4):
            gather_whole(kind, 1, 4).wait_send()

            @pl.when(own_class == kind)
            def _():
                gather_whole(kind, 0, 8).wait_send()
                gather_whole(kind, 0, 7).wait_send()

    def columns(index, width):
        return pl.ds(pl.multiple_of(index * width, width), width)

    def to_lon(hop, s, half, src, dst):
        def swap(step, carry):
            v, lb = step // 2, step % 2
            parts = [
                ysc[pl.ds(pl.multiple_of(k * 32 + lb * 16, 16), 16), columns(v, 128)] for k in range(8)
            ]
            parts = exchange(parts, (1, 2, 4))
            for og in range(8):
                ssc[pl.ds(pl.multiple_of((v * 8 + og) * 32 + lb * 16, 16), 16), :] = parts[og]
            return carry

        repeat(4, swap)

        def pick(step, carry):
            peer = l_peer(step)
            src[s, half, peer_rows(peer, 16), :] = ssc[pl.ds(peer, 16, stride=32), :]
            send_l(hop, s, half, src, dst, peer)
            return carry

        repeat(LN - 1, pick)
        dst[s, half, peer_rows(ml, 16), :] = ssc[pl.ds(ml, 16, stride=32), :]

    def lat_first(s, half):
        whole_z(0, s, half, send0, recv0).wait_recv()
        if s == 0:
            start_z(0, 1, half, send0, recv0)
        cells = jnp.concatenate([recv0[s, half, :, v].reshape(256, 128) for v in range(2)], axis=1)
        ysc[...] = dot(latp[...], cells, NN)
        to_lon(1, s, half, send1, recv1)

    def lon_columns(s, src):
        def turn(c, carry):
            block = jnp.concatenate(
                [src[s, half, peer_rows(c * 4 + i, 16), :] for i in range(4) for half in range(2)], axis=0
            ).T
            high, low = split(block)
            halves[0:128, columns(c, 128)] = high
            halves[128:256, columns(c, 128)] = low
            return carry

        repeat(8, turn)

    def lon_first(s):
        for half in range(2):
            whole_l(1, s, half, send1, recv1).wait_recv()
        lon_columns(s, recv1)

        squares = jnp.zeros((1, 128), F32)
        for n in range(4):
            cols = slice(n * 256, (n + 1) * 256)
            both = dot(halves[:, : (n + 1) * 256], lonfull[cols, : (n + 1) * 256], NT)
            drawn = both[0:128] + both[128:256]
            left = mask[:, cols].astype(F32) * (obs[:, cols] - drawn)
            prior[s, :, cols] = drawn
            resid[s, :, cols] = left
            summed = jnp.sum(left * left, axis=0, keepdims=True)
            squares = squares + summed[:, 0:128] + summed[:, 128:256]
        redsend[s, 0:1, :] = squares

        def halve(n, carry):
            high, low = split(resid[s, :, columns(n, 256)])
            halves[0:128, columns(n, 256)] = high
            halves[128:256, columns(n, 256)] = low
            return carry

        repeat(4, halve)

        for step in range(4):
            n = lax.rem(ml // 8 + step, 4)
            both = dot(halves[...], lonfull[:, columns(n, 256)], NN)
            summed = both[0:128] + both[128:256]
            for part in range(2):
                rows = pl.ds(pl.multiple_of(n * 256 + part * 128, 128), 128)
                send2[s, 0, rows, :] = summed[:, part * 128 : (part + 1) * 128].T.astype(BF16)

            def one(k, carry):
                send_l(2, s, 0, send2, recv2, n * 8 + lax.rem(ml + k, 8))
                return carry

            lax.fori_loop(1 if step == 0 else 0, 8, one, 0, unroll=True)
        recv2[s, 0, peer_rows(ml), :] = send2[s, 0, peer_rows(ml), :]

    def lat_back(s):
        whole_l(2, s, 0, send2, recv2).wait_recv()
        ssc[...] = recv2[s, 0].astype(F32)
        for half in range(2):

            def swap(step, carry):
                v, lb = step // 2, step % 2
                base = lb * 512 + half * 16 + v * 8
                parts = [ssc[pl.ds(base + pg, 16, stride=32), :] for pg in range(8)]
                parts = exchange(parts, (1, 2, 4))
                for k in range(8):
                    rows = pl.ds(pl.multiple_of(k * 32 + lb * 16, 16), 16)
                    xd[rows, columns(v, 128)] = parts[k].astype(BF16)
                return carry

            repeat(4, swap)
            ysc[...] = dot(latqt[...], xd[...], NN)

            def turn(step, carry):
                v, ib = step // 2, step % 2
                parts = [
                    ysc[pl.ds(pl.multiple_of(bb * 16 + ib * 8, 8), 8), columns(v, 128)] for bb in range(16)
                ]
                parts = exchange(parts, (8, 16, 32, 64))
                for h in range(16):
                    tsc[pl.ds(pl.multiple_of((v * 16 + h) * 16 + ib * 8, 8), 8), :] = parts[h]
                return carry

            repeat(4, turn)

            def picked(peer, v):
                return tsc[pl.ds(v * 256 + peer, 16, stride=16), :].astype(BF16)

            def pick(step, carry):
                peer = z_peer(step)
                for v in range(2):
                    send3[s, half, peer, v] = picked(peer, v)
                send_z(3, s, half, send3, recv3, peer)
                return carry

            repeat(ZN - 1, pick)
            for v in range(2):
                recv3[s, half, mz, v] = picked(mz, v)

    quads = {}

    def hours_mix(s, half):
        whole_z(3, s, half, send3, recv3).wait_recv()
        cells = jnp.concatenate([recv3[s, half, :, v].reshape(256, 128) for v in range(2)], axis=1)
        both = dot(hour[...], cells, NN)
        mixed = both[0:256] + both[256:512]
        total = jnp.sum(mixed * cells.astype(F32), axis=0, keepdims=True)
        quads[s, half] = total[:, 0:128] + total[:, 128:256]
        for v in range(2):
            send4[s, half, :, v] = mixed[:, v * 128 : (v + 1) * 128].astype(BF16).reshape(16, 16, 128)
        if half == 1:
            redsend[s, 1:2, :] = quads[s, 0] + quads[s, 1]

            def one(step, carry):
                pltpu.make_async_remote_copy(
                    src_ref=redsend.at[s], dst_ref=redz.at[s, mz],
                    send_sem=send_sem.at[6, s, 0], recv_sem=recv_sem.at[6, s, 0],
                    device_id={"tm": z_peer(step)}, device_id_type=MESH,
                ).start()
                return carry

            lax.fori_loop(0, ZN - 1, one, 0)
            redz[s, mz] = redsend[s]
        start_z(4, s, half, send4, recv4)

    def sums_z_whole(s):
        part = redz.at[s, pl.ds(0, ZN - 1)]
        return pltpu.make_async_remote_copy(
            src_ref=part, dst_ref=part, send_sem=send_sem.at[6, s, 0], recv_sem=recv_sem.at[6, s, 0],
            device_id={"tm": z_peer(0)}, device_id_type=MESH,
        )

    def sums_lon(s):
        sums_z_whole(s).wait_recv()
        redmid[s] = jnp.sum(redz[s], axis=0)

        def one(step, carry):
            pltpu.make_async_remote_copy(
                src_ref=redmid.at[s], dst_ref=redl.at[s, ml],
                send_sem=send_sem.at[7, s, 0], recv_sem=recv_sem.at[7, s, 0],
                device_id={"lon": l_peer(step)}, device_id_type=MESH,
            ).start()
            return carry

        lax.fori_loop(0, LN - 1, one, 0)
        redl[s, ml] = redmid[s]

    def sums_whole(s):
        part = redl.at[s, pl.ds(0, LN - 1)]
        return pltpu.make_async_remote_copy(
            src_ref=part, dst_ref=part, send_sem=send_sem.at[7, s, 0], recv_sem=recv_sem.at[7, s, 0],
            device_id={"lon": l_peer(0)}, device_id_type=MESH,
        )

    def lat_last(s, half):
        whole_z(4, s, half, send4, recv4).wait_recv()

        def widen(i, carry):
            ssc[peer_rows(i), :] = recv4[s, half, i].reshape(32, 128).astype(F32)
            return carry

        repeat(ZN, widen)

        def turn(v, carry):
            parts = [ssc[pl.ds(v * 16 + h, 16, stride=32), :] for h in range(16)]
            parts = exchange(parts, (8, 16, 32, 64))
            for bb in range(16):
                xd[pl.ds(bb * 16, 16), columns(v, 128)] = parts[bb].astype(BF16)
            return carry

        repeat(2, turn)
        ysc[...] = dot(latq[...], xd[...], NN)
        to_lon(5, s, half, send5, recv5)

    def lon_last(s):
        sums_whole(s).wait_recv()
        total = jnp.sum(redl[s], axis=0)
        norm_sq = jnp.sum(total[0:1], axis=1, keepdims=True)
        quad = jnp.sum(total[1:2], axis=1, keepdims=True)
        step_size = norm_sq / (quad + NOISE_VAR * norm_sq)
        for half in range(2):
            whole_l(5, s, half, send5, recv5).wait_recv()
        lon_columns(s, recv5)

        for n in range(4):
            cols = slice(n * 256, (n + 1) * 256)
            both = dot(halves[:, : (n + 1) * 256], lonfull[cols, : (n + 1) * 256], NT)
            applied = both[0:128] + both[128:256]
            left = resid[s, :, cols]
            operated = mask[:, cols].astype(F32) * applied + NOISE_VAR * left
            prior[s, :, cols] += step_size * applied
            resid[s, :, cols] = left - step_size * operated
            for index, (held, result) in enumerate([(prior, post), (resid, nxt)]):
                pltpu.make_async_copy(
                    held.at[s, :, cols], result.at[s, :, cols], local_sem.at[10 + 2 * s + index]
                ).start()

    def results(s):
        return [
            pltpu.make_async_copy(src.at[s], dst.at[s], local_sem.at[10 + 2 * s + index])
            for index, (src, dst) in enumerate([(prior, post), (resid, nxt)])
        ]

    lat_first(0, 0)
    lat_first(0, 1)
    gather_forward()
    gather_finish()
    lon_first(0)
    lat_first(1, 0)
    lat_first(1, 1)
    lat_back(0)
    lon_first(1)
    hours_mix(0, 0)
    lat_back(1)
    hours_mix(0, 1)
    hours_mix(1, 0)
    hours_mix(1, 1)
    lat_last(0, 0)
    lat_last(0, 1)
    sums_lon(0)
    lat_last(1, 0)
    sums_lon(1)
    lon_last(0)
    lat_last(1, 1)
    lon_last(1)

    gather_drain()
    for s in range(2):
        for half in range(2):
            whole_z(0, s, half, send0, recv0).wait_send()
            whole_l(1, s, half, send1, recv1).wait_send()
            whole_z(3, s, half, send3, recv3).wait_send()
            whole_z(4, s, half, send4, recv4).wait_send()
            whole_l(5, s, half, send5, recv5).wait_send()
        whole_l(2, s, 0, send2, recv2).wait_send()
        sums_z_whole(s).wait_send()
        sums_whole(s).wait_send()
        for copy in results(s):
            copy.wait()


def trig(step, period, count, columns):
    angle = 2.0 * np.pi * ((step * np.arange(count)[:, None] * np.arange(columns)[None]) % period) / period
    return np.concatenate([np.cos(angle), np.sin(angle)]).astype(np.float32)


def shards(noise, observed, mask, lat_factor, lon_factor, spectrum):
    periods = noise.shape[3]
    coarse = jnp.asarray(trig(16, 512, 16, 512))
    fine = jnp.asarray(trig(1, 512, 16, 512))
    vmem = pl.BlockSpec(memory_space=pltpu.VMEM)
    hbm = pl.BlockSpec(memory_space=pltpu.HBM)
    zbuf = pltpu.VMEM((2, 2, 16, 2, 16, 128), BF16)
    lbuf = pltpu.VMEM((2, 2, 512, 128), F32)
    lhalf = pltpu.VMEM((2, 1, 1024, 128), BF16)
    scratch = [
        pltpu.VMEM((2, 16, 32, 512), BF16),
        pltpu.VMEM((256, 256), BF16),
        pltpu.VMEM((32, 1024), BF16),
        pltpu.VMEM((32, 512), F32),
        pltpu.VMEM((32, 512), F32),
        pltpu.VMEM((257,), F32),
        pltpu.VMEM((128, 1024), F32),
        pltpu.VMEM((128, 1024), jnp.int32),
        pltpu.VMEM((2, 2, 128, 1024), BF16),
        pltpu.VMEM((2, 256, 1024), BF16),
        pltpu.VMEM((512, 128), F32),
        pltpu.VMEM((256, 256), F32),
        pltpu.VMEM((1024, 128), F32),
        pltpu.VMEM((512, 128), F32),
        pltpu.VMEM((512, 128), F32),
        pltpu.VMEM((256, 256), BF16),
        pltpu.VMEM((256, 256), BF16),
        pltpu.VMEM((256, 256), BF16),
        pltpu.VMEM((512, 256), BF16),
        pltpu.VMEM((1024, 1024), BF16),
        pltpu.VMEM((256, 1024), BF16),
        pltpu.VMEM((256, 256), BF16),
        pltpu.VMEM((2, 128, 1024), F32),
        pltpu.VMEM((2, 128, 1024), F32),
        zbuf, zbuf, lbuf, lbuf, lhalf, lhalf, zbuf, zbuf, zbuf, zbuf, lbuf, lbuf,
        pltpu.VMEM((2, 8, 128), F32),
        pltpu.VMEM((2, 16, 8, 128), F32),
        pltpu.VMEM((2, 8, 128), F32),
        pltpu.VMEM((2, 32, 8, 128), F32),
        pltpu.SemaphoreType.DMA((HOPS, 2, 2)),
        pltpu.SemaphoreType.DMA((HOPS, 2, 2)),
        pltpu.SemaphoreType.DMA((2, 4)),
        pltpu.SemaphoreType.DMA((2, 4)),
        pltpu.SemaphoreType.DMA((14,)),
    ]
    out = jax.ShapeDtypeStruct((2, 128, 1024), F32)
    post, nxt = pl.pallas_call(
        body,
        out_shape=(out, out),
        in_specs=[hbm] * 8,
        out_specs=(hbm, hbm),
        scratch_shapes=scratch,
        compiler_params=pltpu.CompilerParams(
            collective_id=0, has_side_effects=True, vmem_limit_bytes=58 << 20
        ),
        name="posterior",
    )(
        noise, observed.reshape(128, 1024), mask.reshape(128, 1024), lat_factor, lon_factor, spectrum, coarse, fine
    )
    return post.reshape(2, 16, 8, 1024), nxt.reshape(2, 16, 8, 1024)


def solution(mesh):
    return jax.shard_map(
        shards,
        mesh=mesh,
        in_specs=(
            P(None, "tm", "lon", None),
            P("tm", "lon", None),
            P("tm", "lon", None),
            P(),
            P("lon", None),
            P(),
        ),
        out_specs=(P(None, "tm", "lon", None), P(None, "tm", "lon", None)),
        check_vma=False,
    )
```
